32 devices in a mesh: grp: 2 (over y), az: 4 (over z), el: 2 (over x), fq: 2 (over core).
Axes of the slice: x: 2, y: 2, z: 4, core: 2. Of those that a mesh axis runs over, the one named last changes fastest.
Arguments:
- polar: bfloat16 [2, 64, 1024, 768], P(None, ('grp', 'el'), 'az', 'fq'), parts along dimension 1, may hold values from -6 to 6
- band_offset: int32 [1024, 768], P('az', 'fq'), may hold values from -8 to 5, as said below
- tap_count: int32 [1024, 768], P('az', 'fq'), may hold values from 4 to 8
- tap_weight: bfloat16 [8, 1024, 768], P(None, 'az', 'fq'), may hold values from -2.390625 to 2.390625
Outputs:
- image_out: bfloat16 [2, 64, 768, 1024], P(None, ('grp', 'el'), ('az', 'fq')), parts along dimension 1
The draws below stay inside these ranges and needn't reach their ends.
There are 2 independent parts, one for each index of `grp`. The reference program is written for one: setup_inputs(seed, part) draws one part's arguments, and reference() takes and returns one part's arrays. A program takes and returns all parts, laid end to end along the dimension named above; an argument that names none is the same for every part. Nothing has to cross between parts.
Inputs may be any that keep to these rules, and one draw needn't show every extreme that they name: band_offset[j, f] lies between -8 and 9 - tap_count[j, f], so a band reads azimuths j - 8 to j + 8; both ends are reached.
All inputs are finite; a program needn't handle non-finite values.
Results may differ from the reference program's by a relative error of at most 0.0074.
Values may be sent and summed in bfloat16 or wider, within the bound.
A program may use at most 128 MiB of HBM per device.

```python
import math
import jax
import jax.numpy as jnp
from jax import lax

F = 768
A = 1024
E = 32
HW = 8
KT = 8


def band_pair(key):
    base_key = jax.random.fold_in(key, 4711)
    sub_keys = jax.random.split(base_key, 3)
    tap_draw = jax.random.randint(sub_keys[0], (A * F,), KT // 2, KT + 1, dtype=jnp.int32)
    raw_draw = jax.random.randint(sub_keys[1], (A * F,), 0, 1 << 20, dtype=jnp.int32)
    spread = 2 * HW + 2 - tap_draw
    offsets = raw_draw % spread - HW
    chosen = jax.random.randint(sub_keys[2], (3,), 0, A * F, dtype=jnp.int32)
    tap_draw = tap_draw.at[chosen[0]].set(KT)
    offsets = offsets.at[chosen[0]].set(-HW)
    offsets = offsets.at[chosen[1]].set(-HW)
    tap_draw = tap_draw.at[chosen[2]].set(KT // 2)
    offsets = offsets.at[chosen[2]].set(HW + 1 - KT // 2)
    return (offsets.reshape(A, F), tap_draw.reshape(A, F))


def draw_band_offset(key, part):
    return band_pair(key)[0]


def draw_tap_count(key, part):
    return band_pair(key)[1]


def block_scale(stream_key, shape, cuts, low, top_value):
    def one(position, shards_of):
        steps = jax.random.uniform(jax.random.fold_in(jax.random.fold_in(stream_key, 6), position), (shards_of,), jnp.float32, low / len(cuts), top_value / len(cuts))
        return jnp.repeat(jnp.exp(steps), shape[position] // shards_of).reshape((-1,) + (1,) * (len(shape) - position - 1))

    level = one(*cuts[0])
    for cut in cuts[1:]:
        level = level * one(*cut)
    return level


def normal_values(stream_key, dims, scale, bound, cuts=(), kind=jnp.bfloat16):
    array = jax.random.normal(stream_key, dims, jnp.float32) * scale
    if len(cuts) > 0:
        array = block_scale(stream_key, dims, cuts, -0.22, 0.18) * array
    return jnp.clip(array, min=-bound, max=bound).astype(kind)


def setup_inputs(seed: int = 0, part: int = 0) -> dict:
    streams_of = jax.random.split(jax.random.key(seed), 5)
    own_keys = jax.random.split(jax.random.fold_in(streams_of[4], part), 5)
    polar = normal_values(own_keys[0], (2, E, A, F), 1.0, 6.0, ((1, 2), (2, 4), (3, 2)))
    band_offset = draw_band_offset(jax.random.fold_in(streams_of[4], 71), part)
    tap_count = draw_tap_count(jax.random.fold_in(streams_of[4], 71), part)
    tap_weight = normal_values(streams_of[3], (KT, A, F), 0.4, 2.390625, ((1, 4), (2, 2)))
    return {"polar": polar, "band_offset": band_offset, "tap_count": tap_count, "tap_weight": tap_weight}


def table_pair(row_ids, col_ids, length):
    product = row_ids[:, None] * col_ids[None, :] % length
    angle = product.astype(jnp.float32) * (2.0 * math.pi / length)
    return (jnp.cos(angle).astype(jnp.bfloat16), jnp.sin(angle).astype(jnp.bfloat16))

def complex_dot(real_in, imag_in, cos_tab, sin_tab):
    real_wide = real_in.astype(jnp.float32)
    imag_wide = imag_in.astype(jnp.float32)
    cos_wide = cos_tab.astype(jnp.float32)
    sin_wide = sin_tab.astype(jnp.float32)
    high = lax.Precision.HIGHEST
    real_out = jnp.dot(real_wide, cos_wide, precision=high) - jnp.dot(imag_wide, sin_wide, precision=high)
    imag_out = jnp.dot(real_wide, sin_wide, precision=high) + jnp.dot(imag_wide, cos_wide, precision=high)
    return (real_out, imag_out)

def reference(polar, band_offset, tap_count, tap_weight):
    freq_ids = jnp.arange(F, dtype=jnp.int32)
    azim_ids = jnp.arange(A, dtype=jnp.int32)
    elev_ids = jnp.arange(E, dtype=jnp.int32)
    cos_f, sin_f = table_pair(freq_ids, freq_ids, F)
    cos_a, sin_a = table_pair(azim_ids, azim_ids, A)
    cos_e, sin_e = table_pair(elev_ids, elev_ids, E)
    weights = tap_weight.astype(jnp.float32)
    column_ids = azim_ids[:, None]

    def one_cut(cut_slab):
        padded = jnp.pad(cut_slab.astype(jnp.float32), ((0, 0), (HW, HW), (0, 0)))
        accumulated = jnp.zeros((2, A, F), jnp.float32)
        for tap_index in range(KT):
            source_index = jnp.minimum(column_ids + HW + band_offset + tap_index, A + 2 * HW - 1).astype(jnp.int32)
            gathered = jnp.take_along_axis(padded, jnp.broadcast_to(source_index[None], (2, A, F)), axis=1)
            accumulated = accumulated + jnp.where((tap_index < tap_count)[None], weights[tap_index][None] * gathered, 0.0)
        interpolated = accumulated.astype(jnp.bfloat16)
        range_real, range_imag = complex_dot(interpolated[0], interpolated[1], cos_f, sin_f)
        ranged = (jnp.stack([range_real, range_imag]) * (1.0 / math.sqrt(F))).astype(jnp.bfloat16)
        transposed = jnp.swapaxes(ranged, 1, 2)
        cross_real, cross_imag = complex_dot(transposed[0], transposed[1], cos_a, sin_a)
        return (jnp.stack([cross_real, cross_imag]) * (1.0 / math.sqrt(A))).astype(jnp.bfloat16)
    crossed = lax.map(one_cut, jnp.moveaxis(polar, 1, 0))
    flattened = crossed.astype(jnp.float32).reshape(E, 2, F * A)
    cos_wide = cos_e.astype(jnp.float32)
    sin_wide = sin_e.astype(jnp.float32)
    high = lax.Precision.HIGHEST
    height_real = jnp.einsum('eh,ex->hx', cos_wide, flattened[:, 0], precision=high) - jnp.einsum('eh,ex->hx', sin_wide, flattened[:, 1], precision=high)
    height_imag = jnp.einsum('eh,ex->hx', sin_wide, flattened[:, 0], precision=high) + jnp.einsum('eh,ex->hx', cos_wide, flattened[:, 1], precision=high)
    image_out = (jnp.stack([height_real, height_imag]) * (1.0 / math.sqrt(E))).astype(jnp.bfloat16)
    return image_out.reshape(2, E, F, A)
```

```python
import math

import jax
import jax.numpy as jnp
from jax import lax
from jax.experimental import pallas as pl
from jax.experimental.pallas import tpu as pltpu
from jax.sharding import PartitionSpec as P

F = 768
A = 1024
E = 32
HW = 8
KT = 8
LANES = 128
GROUP = 16
CHUNKS = 4


def with_halo(cells, sides, width):
    for axis, dim in sides:
        count = lax.axis_size(axis)
        ends = count - 1
        head = lax.slice_in_dim(cells, 0, width, axis=dim)
        tail = lax.slice_in_dim(cells, cells.shape[dim] - width, cells.shape[dim], axis=dim)
        cells = jnp.concatenate(
            [
                lax.ppermute(tail, axis, [(i, (i + 1) % count) for i in range(ends)]),
                cells,
                lax.ppermute(head, axis, [((i + 1) % count, i) for i in range(ends)]),
            ],
            axis=dim,
        )
    return cells


def table_pair(row_ids, col_ids, length):
    product = row_ids[:, None] * col_ids[None, :] % length
    angle = product.astype(jnp.float32) * (2.0 * math.pi / length)
    return (jnp.cos(angle).astype(jnp.bfloat16), jnp.sin(angle).astype(jnp.bfloat16))


def on_device(polar, band_offset, tap_count, tap_weight):
    shape_all = polar.shape
    col_count = shape_all[2]
    freq_count = shape_all[3]
    az_count = lax.axis_size("az")
    fq_count = lax.axis_size("fq")
    el_count = lax.axis_size("el")
    padded = with_halo(polar, (("az", 2),), HW)
    window = col_count + 2 * HW
    column = jnp.arange(col_count, dtype=jnp.int32)[:, None]
    position = jnp.arange(window, dtype=jnp.int32)[None, :, None]
    band_matrix = jnp.zeros((col_count, window, freq_count), jnp.bfloat16)
    for tap_index in range(KT):
        reach = column + HW + band_offset + tap_index
        matches = (position == reach[:, None, :]) & (tap_index < tap_count)[:, None, :]
        band_matrix = jnp.where(matches, tap_weight[tap_index][:, None, :], band_matrix)
    interpolated = jnp.einsum(
        "jaf,ceaf->cejf", band_matrix, padded, preferred_element_type=jnp.float32
    ).astype(jnp.bfloat16)
    fq_index = lax.axis_index("fq")
    bin_count = F // (fq_count * az_count)
    az_block = jnp.arange(az_count, dtype=jnp.int32)[:, None]
    bin_local = jnp.arange(bin_count, dtype=jnp.int32)[None, :]
    range_bins = ((az_block * fq_count + fq_index) * bin_count + bin_local).reshape(-1)
    cos_f, sin_f = table_pair(jnp.arange(F, dtype=jnp.int32), range_bins, F)
    shard_piece = lax.all_gather(interpolated, "fq", axis=3, tiled=True)
    cos_rows = cos_f
    sin_rows = sin_f
    real_part = jnp.einsum(
        "ejf,fk->ekj", shard_piece[0], cos_rows, preferred_element_type=jnp.float32
    ) - jnp.einsum("ejf,fk->ekj", shard_piece[1], sin_rows, preferred_element_type=jnp.float32)
    imag_part = jnp.einsum(
        "ejf,fk->ekj", shard_piece[0], sin_rows, preferred_element_type=jnp.float32
    ) + jnp.einsum("ejf,fk->ekj", shard_piece[1], cos_rows, preferred_element_type=jnp.float32)
    summed = jnp.stack([real_part, imag_part])
    ranged = (summed * (1.0 / math.sqrt(F))).astype(jnp.bfloat16)
    azim_ids = jnp.arange(A, dtype=jnp.int32)
    cos_a, sin_a = table_pair(azim_ids, azim_ids, A)
    block_data = lax.all_to_all(ranged, "az", split_axis=2, concat_axis=3, tiled=True)
    real_part = jnp.einsum(
        "ekj,jm->ekm", block_data[0], cos_a, preferred_element_type=jnp.float32
    ) - jnp.einsum("ekj,jm->ekm", block_data[1], sin_a, preferred_element_type=jnp.float32)
    imag_part = jnp.einsum(
        "ekj,jm->ekm", block_data[0], sin_a, preferred_element_type=jnp.float32
    ) + jnp.einsum("ekj,jm->ekm", block_data[1], cos_a, preferred_element_type=jnp.float32)
    crossed = (jnp.stack([real_part, imag_part]) * (1.0 / math.sqrt(A))).astype(jnp.bfloat16)
    elev_ids = jnp.arange(E, dtype=jnp.int32)
    el_index = lax.axis_index("el")
    height_count = E // el_count
    height_rows = el_index * height_count + jnp.arange(height_count, dtype=jnp.int32)
    cos_e, sin_e = table_pair(elev_ids, height_rows, E)
    shard_piece = lax.all_gather(crossed, "el", axis=1, tiled=True)
    cos_rows = cos_e
    sin_rows = sin_e
    real_part = jnp.einsum(
        "eh,ekm->hkm", cos_rows, shard_piece[0], preferred_element_type=jnp.float32
    ) - jnp.einsum("eh,ekm->hkm", sin_rows, shard_piece[1], preferred_element_type=jnp.float32)
    imag_part = jnp.einsum(
        "eh,ekm->hkm", sin_rows, shard_piece[0], preferred_element_type=jnp.float32
    ) + jnp.einsum("eh,ekm->hkm", cos_rows, shard_piece[1], preferred_element_type=jnp.float32)
    totals = jnp.stack([real_part, imag_part])
    image_out = (totals * (1.0 / math.sqrt(E))).astype(jnp.bfloat16)
    return image_out


def trig_pair(row_ids, col_ids, length, split=32):
    fine = jnp.arange(split, dtype=jnp.int32)

    def small(factor):
        product = (factor[:, None] * col_ids[None, :]) % length
        angle = product.astype(jnp.float32) * (2.0 * math.pi / length)
        return jnp.cos(angle), jnp.sin(angle)

    block = row_ids.shape[0] // split
    starts = row_ids.reshape(block, split)[:, 0]
    low_cos, low_sin = small(fine)
    high_cos, high_sin = small(starts)
    low_cos, low_sin, high_cos, high_sin = lax.optimization_barrier(
        (low_cos, low_sin, high_cos, high_sin)
    )
    shape = (block * split, col_ids.shape[0])
    cos_t = high_cos[:, None] * low_cos[None] - high_sin[:, None] * low_sin[None]
    sin_t = high_sin[:, None] * low_cos[None] + high_cos[:, None] * low_sin[None]
    return (
        cos_t.reshape(shape).astype(jnp.bfloat16),
        sin_t.reshape(shape).astype(jnp.bfloat16),
    )


def cost(flops, moved):
    return pl.CostEstimate(flops=int(flops), bytes_accessed=int(moved), transcendentals=0)


def params():
    return pltpu.CompilerParams(vmem_limit_bytes=48 * 1024 * 1024)


def weights_body(off_ref, cnt_ref, tap_ref, w_ref):
    rows = 16

    @pl.loop(0, off_ref.shape[0] // rows)
    def _(step):
        at = pl.ds(pl.multiple_of(step * rows, rows), rows)
        off = off_ref[at, :]
        cnt = cnt_ref[at, :]
        taps = [
            jnp.where(t < cnt, tap_ref[t, at, :].astype(jnp.float32), 0.0) for t in range(KT)
        ]
        for d in range(2 * HW + 1):
            rel = (d - HW) - off
            acc = jnp.zeros(off.shape, jnp.float32)
            for t in range(KT):
                acc = jnp.where(rel == t, taps[t], acc)
            w_ref[d, at, :] = acc.astype(jnp.bfloat16)


def band_weights(band_offset, tap_count, tap_weight):
    cols, freqs = band_offset.shape
    taps = 2 * HW + 1
    return pl.pallas_call(
        weights_body,
        out_shape=jax.ShapeDtypeStruct((taps, cols, freqs), jnp.bfloat16),
        grid=(freqs // LANES,),
        in_specs=[
            pl.BlockSpec((cols, LANES), lambda i: (0, i)),
            pl.BlockSpec((cols, LANES), lambda i: (0, i)),
            pl.BlockSpec((KT, cols, LANES), lambda i: (0, 0, i)),
        ],
        out_specs=pl.BlockSpec((taps, cols, LANES), lambda i: (0, 0, i)),
        compiler_params=params(),
        cost_estimate=cost(10**9, 6 * 10**6),
        name="weights",
    )(band_offset, tap_count, tap_weight)


def interp_body(x_ref, l_ref, r_ref, w_ref, o_ref, buf):
    cuts = x_ref.shape[1]
    cols = x_ref.shape[2]
    rows = 16
    for c in range(2):
        for e in range(cuts):
            p = c * cuts + e
            buf[p, 0:HW, :] = l_ref[c, e].astype(jnp.float32)
            buf[p, HW : HW + cols, :] = x_ref[c, e].astype(jnp.float32)
            buf[p, HW + cols : 2 * HW + cols, :] = r_ref[c, e].astype(jnp.float32)

    @pl.loop(0, cols // rows)
    def _(step):
        base = pl.multiple_of(step * rows, rows)
        weights = [
            w_ref[d, pl.ds(base, rows), :].astype(jnp.float32) for d in range(2 * HW + 1)
        ]
        for c in range(2):
            for e in range(cuts):
                p = c * cuts + e
                acc = weights[0] * buf[p, pl.ds(base, rows), :]
                for d in range(1, 2 * HW + 1):
                    acc = acc + weights[d] * buf[p, pl.ds(base + d, rows), :]
                o_ref[c, e, pl.ds(base, rows), :] = acc.astype(jnp.bfloat16)


def interpolate(polar, left, right, weights, chunk, cuts):
    _, _, cols, freqs = polar.shape
    taps = 2 * HW + 1
    return pl.pallas_call(
        interp_body,
        out_shape=jax.ShapeDtypeStruct((2, cuts, cols, freqs), jnp.bfloat16),
        grid=(freqs // LANES,),
        in_specs=[
            pl.BlockSpec((2, cuts, cols, LANES), lambda i: (0, chunk, 0, i)),
            pl.BlockSpec((2, cuts, HW, LANES), lambda i: (0, chunk, 0, i)),
            pl.BlockSpec((2, cuts, HW, LANES), lambda i: (0, chunk, 0, i)),
            pl.BlockSpec((taps, cols, LANES), lambda i: (0, 0, i)),
        ],
        out_specs=pl.BlockSpec((2, cuts, cols, LANES), lambda i: (0, 0, 0, i)),
        scratch_shapes=[pltpu.VMEM((2 * cuts, cols + 2 * HW, LANES), jnp.float32)],
        compiler_params=params(),
        cost_estimate=cost(10**9, 6 * 10**6),
        name="interp",
    )(polar, left, right, weights)


def range_body(own_ref, par_ref, tab_ref, *rest):
    outs = rest[:-1]
    xs = rest[-1]
    half = own_ref.shape[3]
    for c in range(2):
        xs[c, :, 0:half] = own_ref[c, 0]
        xs[c, :, half:] = par_ref[c, 0]
    dims = (((1,), (1,)), ((), ()))
    table = tab_ref[...]
    from_real = lax.dot_general(table, xs[0], dims, preferred_element_type=jnp.float32)
    from_imag = lax.dot_general(table, xs[1], dims, preferred_element_type=jnp.float32)
    bins = table.shape[0] // 2
    scale = 1.0 / math.sqrt(F)
    real = ((from_real[:bins] - from_imag[bins:]) * scale).astype(jnp.bfloat16)
    imag = ((from_real[bins:] + from_imag[:bins]) * scale).astype(jnp.bfloat16)
    size = bins // len(outs)
    for s, out in enumerate(outs):
        out[0, 0] = real[s * size : (s + 1) * size]
        out[1, 0] = imag[s * size : (s + 1) * size]


def range_transform(own, partner, table, pieces):
    _, cuts, cols, half = own.shape
    bins = table.shape[0] // 2 // pieces
    spec = pl.BlockSpec((2, 1, cols, half), lambda i: (0, i, 0, 0))
    return pl.pallas_call(
        range_body,
        out_shape=[jax.ShapeDtypeStruct((2, cuts, bins, cols), jnp.bfloat16)] * pieces,
        grid=(cuts,),
        in_specs=[spec, spec, pl.BlockSpec(table.shape, lambda i: (0, 0))],
        out_specs=[pl.BlockSpec((2, 1, bins, cols), lambda i: (0, i, 0, 0))] * pieces,
        scratch_shapes=[pltpu.VMEM((2, cols, 2 * half), jnp.bfloat16)],
        compiler_params=params(),
        cost_estimate=cost(4 * table.size * cuts * cols, 6 * 10**6),
        name="range_dft",
    )(own, partner, table)


def cross_body(*refs):
    pieces = len(refs) - 4
    cos_ref, sin_ref, out_ref, lhs = refs[pieces:]
    _, cuts, bins, cols = refs[0].shape

    @pl.when(pl.program_id(0) == 0)
    def _():
        for s in range(pieces):
            block = refs[s][...].reshape(2 * cuts * bins, cols)
            lhs[:, s * cols : (s + 1) * cols] = block

    left = lhs[...]
    by_cos = jnp.dot(left, cos_ref[...], preferred_element_type=jnp.float32)
    by_sin = jnp.dot(left, sin_ref[...], preferred_element_type=jnp.float32)
    rows = cuts * bins
    scale = 1.0 / math.sqrt(A)
    shape = (cuts, bins, cos_ref.shape[1])
    real = (by_cos[:rows] - by_sin[rows:]) * scale
    imag = (by_sin[:rows] + by_cos[rows:]) * scale
    out_ref[0] = real.astype(jnp.bfloat16).reshape(shape)
    out_ref[1] = imag.astype(jnp.bfloat16).reshape(shape)


def cross_transform(pieces, cos_a, sin_a):
    _, cuts, bins, cols = pieces[0].shape
    depth, width = cos_a.shape
    tile = 256
    whole = pl.BlockSpec((2, cuts, bins, cols), lambda i: (0, 0, 0, 0))
    table = pl.BlockSpec((depth, tile), lambda i: (0, i))
    return pl.pallas_call(
        cross_body,
        out_shape=jax.ShapeDtypeStruct((2, cuts, bins, width), jnp.bfloat16),
        grid=(width // tile,),
        in_specs=[whole] * len(pieces) + [table, table],
        out_specs=pl.BlockSpec((2, cuts, bins, tile), lambda i: (0, 0, 0, i)),
        scratch_shapes=[pltpu.VMEM((2 * cuts * bins, depth), jnp.bfloat16)],
        compiler_params=params(),
        cost_estimate=cost(8 * cuts * bins * depth * width, 8 * 10**6),
        name="cross_dft",
    )(*pieces, cos_a, sin_a)


def height_body(*refs):
    tab_ref, out_ref, data = refs[-3:]
    at = 0
    for ref in refs[:-3]:
        parts, cuts, rows, width = ref.shape
        size = parts * cuts * rows
        data[at : at + size, :] = ref[...].reshape(size, width)
        at += size
    parts, heights, rows, width = out_ref.shape
    scale = 1.0 / math.sqrt(E)
    tile = 256
    for t in range(width // tile):
        cols = slice(t * tile, (t + 1) * tile)
        total = jnp.dot(tab_ref[...], data[:, cols], preferred_element_type=jnp.float32)
        total = (total * scale).astype(jnp.bfloat16)
        out_ref[:, :, :, cols] = total.reshape(parts, heights, rows, tile)


def height_transform(chunks, table, heights):
    bins, width = chunks[0].shape[2:]
    specs = [
        pl.BlockSpec((2, x.shape[1], GROUP, width), lambda i: (0, 0, i, 0)) for x in chunks
    ]
    return pl.pallas_call(
        height_body,
        out_shape=jax.ShapeDtypeStruct((2, heights, bins, width), jnp.bfloat16),
        grid=(bins // GROUP,),
        in_specs=specs + [pl.BlockSpec(table.shape, lambda i: (0, 0))],
        out_specs=pl.BlockSpec((2, heights, GROUP, width), lambda i: (0, 0, i, 0)),
        scratch_shapes=[pltpu.VMEM((table.shape[1], width), jnp.bfloat16)],
        compiler_params=params(),
        cost_estimate=cost(2 * table.size * width * (bins // GROUP), 2 * 10**7),
        name="height_dft",
    )(*chunks, table)


def height_table(height_ids, elev_ids):
    cos_e, sin_e = table_pair(height_ids, elev_ids.reshape(-1), E)
    shape = (height_ids.shape[0],) + elev_ids.shape
    cos_e = cos_e.reshape(shape)
    sin_e = sin_e.reshape(shape)
    real = jnp.stack([cos_e, -sin_e], axis=2)
    imag = jnp.stack([sin_e, cos_e], axis=2)
    small = jnp.stack([real, imag]).reshape(2 * shape[0], 2 * elev_ids.size)
    eye = jnp.eye(GROUP, dtype=jnp.bfloat16)
    full = small[:, None, :, None] * eye[None, :, None, :]
    return full.reshape(small.shape[0] * GROUP, small.shape[1] * GROUP)


def pipelined(polar, band_offset, tap_count, tap_weight):
    _, e_here, col_count, freq_count = polar.shape
    az_count = lax.axis_size("az")
    fq_count = lax.axis_size("fq")
    el_count = lax.axis_size("el")
    az, fq, el = (lax.axis_index(name) for name in ("az", "fq", "el"))
    bins = F // (fq_count * az_count)
    heights = E // el_count
    cuts = e_here // CHUNKS
    ends = az_count - 1
    left = lax.ppermute(
        polar[:, :, col_count - HW :], "az", [(i, i + 1) for i in range(ends)]
    )
    right = lax.ppermute(polar[:, :, :HW], "az", [(i + 1, i) for i in range(ends)])
    weights = band_weights(band_offset, tap_count, tap_weight)

    shifts = jnp.arange(az_count, dtype=jnp.int32)
    targets = (az + shifts) % az_count
    local = jnp.arange(bins, dtype=jnp.int32)
    range_ids = ((targets[:, None] * fq_count + fq) * bins + local[None]).reshape(-1)
    f_local = jnp.arange(freq_count, dtype=jnp.int32)
    freq_ids = jnp.concatenate([fq * freq_count + f_local, (1 - fq) * freq_count + f_local])
    cos_f, sin_f = trig_pair(range_ids, freq_ids, F)
    range_table = jnp.concatenate([cos_f, sin_f])

    sources = (az - shifts) % az_count
    col_local = jnp.arange(col_count, dtype=jnp.int32)
    azim_ids = (sources[:, None] * col_count + col_local[None]).reshape(-1)
    cos_a, sin_a = trig_pair(azim_ids, jnp.arange(A, dtype=jnp.int32), A)

    own = []
    passed = [[] for _ in range(1, el_count)]
    for chunk in range(CHUNKS):
        mixed = interpolate(polar, left, right, weights, chunk, cuts)
        partner = lax.ppermute(mixed, "fq", [(0, 1), (1, 0)])
        pieces = range_transform(mixed, partner, range_table, az_count)
        pieces = [pieces[0]] + [
            lax.ppermute(pieces[s], "az", [(i, (i + s) % az_count) for i in range(az_count)])
            for s in range(1, az_count)
        ]
        crossed = cross_transform(pieces, cos_a, sin_a)
        own.append(crossed)
        for s in range(1, el_count):
            passed[s - 1].append(
                lax.ppermute(crossed, "el", [(i, (i + s) % el_count) for i in range(el_count)])
            )

    height_ids = el * heights + jnp.arange(heights, dtype=jnp.int32)
    el_sources = (el - jnp.arange(el_count, dtype=jnp.int32)) % el_count
    elev_ids = el_sources[:, None] * e_here + jnp.arange(e_here, dtype=jnp.int32)[None]
    table = height_table(height_ids, elev_ids.reshape(el_count * CHUNKS, cuts))
    return height_transform(own + sum(passed, []), table, heights)


def pick(polar, band_offset, tap_count, tap_weight):
    _, e_here, col_count, freq_count = polar.shape
    bins = F // (lax.axis_size("fq") * lax.axis_size("az"))
    fits = (
        lax.axis_size("fq") == 2
        and lax.axis_size("az") <= 4
        and e_here % CHUNKS == 0
        and bins % 32 == 0
        and col_count % LANES == 0
        and freq_count % LANES == 0
    )
    plan = pipelined if fits else on_device
    return plan(polar, band_offset, tap_count, tap_weight)


def solution(mesh):
    in_specs = (
        P(None, ("grp", "el"), "az", "fq"),
        P("az", "fq"),
        P("az", "fq"),
        P(None, "az", "fq"),
    )
    out_specs = P(None, ("grp", "el"), ("az", "fq"), None)
    return jax.shard_map(
        pick, mesh=mesh, in_specs=in_specs, out_specs=out_specs, check_vma=False
    )
```

```python
import functools
import math

import jax
import jax.numpy as jnp
from jax import lax
from jax.experimental import pallas as pl
from jax.experimental.pallas import tpu as pltpu
from jax.sharding import PartitionSpec as P

F = 768
A = 1024
E = 32
HW = 8
KT = 8
LANES = 128
GROUP = 16
CUTS = (4, 4, 4, 4)
EARLY = 2


def with_halo(cells, sides, width):
    for axis, dim in sides:
        count = lax.axis_size(axis)
        ends = count - 1
        head = lax.slice_in_dim(cells, 0, width, axis=dim)
        tail = lax.slice_in_dim(cells, cells.shape[dim] - width, cells.shape[dim], axis=dim)
        cells = jnp.concatenate(
            [
                lax.ppermute(tail, axis, [(i, (i + 1) % count) for i in range(ends)]),
                cells,
                lax.ppermute(head, axis, [((i + 1) % count, i) for i in range(ends)]),
            ],
            axis=dim,
        )
    return cells


def table_pair(row_ids, col_ids, length):
    product = row_ids[:, None] * col_ids[None, :] % length
    angle = product.astype(jnp.float32) * (2.0 * math.pi / length)
    return (jnp.cos(angle).astype(jnp.bfloat16), jnp.sin(angle).astype(jnp.bfloat16))


def on_device(polar, band_offset, tap_count, tap_weight):
    shape_all = polar.shape
    col_count = shape_all[2]
    freq_count = shape_all[3]
    az_count = lax.axis_size("az")
    fq_count = lax.axis_size("fq")
    el_count = lax.axis_size("el")
    padded = with_halo(polar, (("az", 2),), HW)
    window = col_count + 2 * HW
    column = jnp.arange(col_count, dtype=jnp.int32)[:, None]
    position = jnp.arange(window, dtype=jnp.int32)[None, :, None]
    band_matrix = jnp.zeros((col_count, window, freq_count), jnp.bfloat16)
    for tap_index in range(KT):
        reach = column + HW + band_offset + tap_index
        matches = (position == reach[:, None, :]) & (tap_index < tap_count)[:, None, :]
        band_matrix = jnp.where(matches, tap_weight[tap_index][:, None, :], band_matrix)
    interpolated = jnp.einsum(
        "jaf,ceaf->cejf", band_matrix, padded, preferred_element_type=jnp.float32
    ).astype(jnp.bfloat16)
    fq_index = lax.axis_index("fq")
    bin_count = F // (fq_count * az_count)
    az_block = jnp.arange(az_count, dtype=jnp.int32)[:, None]
    bin_local = jnp.arange(bin_count, dtype=jnp.int32)[None, :]
    range_bins = ((az_block * fq_count + fq_index) * bin_count + bin_local).reshape(-1)
    cos_f, sin_f = table_pair(jnp.arange(F, dtype=jnp.int32), range_bins, F)
    shard_piece = lax.all_gather(interpolated, "fq", axis=3, tiled=True)
    cos_rows = cos_f
    sin_rows = sin_f
    real_part = jnp.einsum(
        "ejf,fk->ekj", shard_piece[0], cos_rows, preferred_element_type=jnp.float32
    ) - jnp.einsum("ejf,fk->ekj", shard_piece[1], sin_rows, preferred_element_type=jnp.float32)
    imag_part = jnp.einsum(
        "ejf,fk->ekj", shard_piece[0], sin_rows, preferred_element_type=jnp.float32
    ) + jnp.einsum("ejf,fk->ekj", shard_piece[1], cos_rows, preferred_element_type=jnp.float32)
    summed = jnp.stack([real_part, imag_part])
    ranged = (summed * (1.0 / math.sqrt(F))).astype(jnp.bfloat16)
    azim_ids = jnp.arange(A, dtype=jnp.int32)
    cos_a, sin_a = table_pair(azim_ids, azim_ids, A)
    block_data = lax.all_to_all(ranged, "az", split_axis=2, concat_axis=3, tiled=True)
    real_part = jnp.einsum(
        "ekj,jm->ekm", block_data[0], cos_a, preferred_element_type=jnp.float32
    ) - jnp.einsum("ekj,jm->ekm", block_data[1], sin_a, preferred_element_type=jnp.float32)
    imag_part = jnp.einsum(
        "ekj,jm->ekm", block_data[0], sin_a, preferred_element_type=jnp.float32
    ) + jnp.einsum("ekj,jm->ekm", block_data[1], cos_a, preferred_element_type=jnp.float32)
    crossed = (jnp.stack([real_part, imag_part]) * (1.0 / math.sqrt(A))).astype(jnp.bfloat16)
    elev_ids = jnp.arange(E, dtype=jnp.int32)
    el_index = lax.axis_index("el")
    height_count = E // el_count
    height_rows = el_index * height_count + jnp.arange(height_count, dtype=jnp.int32)
    cos_e, sin_e = table_pair(elev_ids, height_rows, E)
    shard_piece = lax.all_gather(crossed, "el", axis=1, tiled=True)
    cos_rows = cos_e
    sin_rows = sin_e
    real_part = jnp.einsum(
        "eh,ekm->hkm", cos_rows, shard_piece[0], preferred_element_type=jnp.float32
    ) - jnp.einsum("eh,ekm->hkm", sin_rows, shard_piece[1], preferred_element_type=jnp.float32)
    imag_part = jnp.einsum(
        "eh,ekm->hkm", sin_rows, shard_piece[0], preferred_element_type=jnp.float32
    ) + jnp.einsum("eh,ekm->hkm", cos_rows, shard_piece[1], preferred_element_type=jnp.float32)
    totals = jnp.stack([real_part, imag_part])
    image_out = (totals * (1.0 / math.sqrt(E))).astype(jnp.bfloat16)
    return image_out


def trig_pair(row_ids, col_ids, length, split=32):
    fine = jnp.arange(split, dtype=jnp.int32)

    def small(factor):
        product = (factor[:, None] * col_ids[None, :]) % length
        angle = product.astype(jnp.float32) * (2.0 * math.pi / length)
        return jnp.cos(angle), jnp.sin(angle)

    block = row_ids.shape[0] // split
    starts = row_ids.reshape(block, split)[:, 0]
    low_cos, low_sin = small(fine)
    high_cos, high_sin = small(starts)
    low_cos, low_sin, high_cos, high_sin = lax.optimization_barrier(
        (low_cos, low_sin, high_cos, high_sin)
    )
    shape = (block * split, col_ids.shape[0])
    cos_t = high_cos[:, None] * low_cos[None] - high_sin[:, None] * low_sin[None]
    sin_t = high_sin[:, None] * low_cos[None] + high_cos[:, None] * low_sin[None]
    return (
        cos_t.reshape(shape).astype(jnp.bfloat16),
        sin_t.reshape(shape).astype(jnp.bfloat16),
    )


def cost(flops, moved):
    return pl.CostEstimate(flops=int(flops), bytes_accessed=int(moved), transcendentals=0)


def params():
    return pltpu.CompilerParams(vmem_limit_bytes=48 * 1024 * 1024)


def weights_body(off_ref, cnt_ref, tap_ref, w_ref):
    rows = 16

    @pl.loop(0, off_ref.shape[0] // rows)
    def _(step):
        at = pl.ds(pl.multiple_of(step * rows, rows), rows)
        off = off_ref[at, :]
        cnt = cnt_ref[at, :]
        taps = [
            jnp.where(t < cnt, tap_ref[t, at, :].astype(jnp.float32), 0.0) for t in range(KT)
        ]
        for d in range(2 * HW + 1):
            rel = (d - HW) - off
            acc = jnp.zeros(off.shape, jnp.float32)
            for t in range(KT):
                acc = jnp.where(rel == t, taps[t], acc)
            w_ref[d, at, :] = acc.astype(jnp.bfloat16)


def band_weights(band_offset, tap_count, tap_weight):
    cols, freqs = band_offset.shape
    taps = 2 * HW + 1
    return pl.pallas_call(
        weights_body,
        out_shape=jax.ShapeDtypeStruct((taps, cols, freqs), jnp.bfloat16),
        grid=(freqs // LANES,),
        in_specs=[
            pl.BlockSpec((cols, LANES), lambda i: (0, i)),
            pl.BlockSpec((cols, LANES), lambda i: (0, i)),
            pl.BlockSpec((KT, cols, LANES), lambda i: (0, 0, i)),
        ],
        out_specs=pl.BlockSpec((taps, cols, LANES), lambda i: (0, 0, i)),
        compiler_params=params(),
        cost_estimate=cost(10**9, 6 * 10**6),
        name="weights",
    )(band_offset, tap_count, tap_weight)


def interp_body(x_ref, l_ref, r_ref, w_ref, o_ref, buf):
    cuts = x_ref.shape[1]
    cols = x_ref.shape[2]
    rows = 16
    for c in range(2):
        for e in range(cuts):
            p = c * cuts + e
            buf[p, 0:HW, :] = l_ref[c, e].astype(jnp.float32)
            buf[p, HW : HW + cols, :] = x_ref[c, e].astype(jnp.float32)
            buf[p, HW + cols : 2 * HW + cols, :] = r_ref[c, e].astype(jnp.float32)

    @pl.loop(0, cols // rows)
    def _(step):
        base = pl.multiple_of(step * rows, rows)
        weights = [
            w_ref[d, pl.ds(base, rows), :].astype(jnp.float32) for d in range(2 * HW + 1)
        ]
        for c in range(2):
            for e in range(cuts):
                p = c * cuts + e
                acc = weights[0] * buf[p, pl.ds(base, rows), :]
                for d in range(1, 2 * HW + 1):
                    acc = acc + weights[d] * buf[p, pl.ds(base + d, rows), :]
                o_ref[c, e, pl.ds(base, rows), :] = acc.astype(jnp.bfloat16)


def interpolate(polar, left, right, weights, first, cuts):
    _, _, cols, freqs = polar.shape
    taps = 2 * HW + 1
    chunk = first // cuts
    return pl.pallas_call(
        interp_body,
        out_shape=jax.ShapeDtypeStruct((2, cuts, cols, freqs), jnp.bfloat16),
        grid=(freqs // LANES,),
        in_specs=[
            pl.BlockSpec((2, cuts, cols, LANES), lambda i: (0, chunk, 0, i)),
            pl.BlockSpec((2, cuts, HW, LANES), lambda i: (0, chunk, 0, i)),
            pl.BlockSpec((2, cuts, HW, LANES), lambda i: (0, chunk, 0, i)),
            pl.BlockSpec((taps, cols, LANES), lambda i: (0, 0, i)),
        ],
        out_specs=pl.BlockSpec((2, cuts, cols, LANES), lambda i: (0, 0, 0, i)),
        scratch_shapes=[pltpu.VMEM((2 * cuts, cols + 2 * HW, LANES), jnp.float32)],
        compiler_params=params(),
        cost_estimate=cost(10**9, 6 * 10**6),
        name="interp",
    )(polar, left, right, weights)


def range_body(own_ref, par_ref, tab_ref, *rest):
    outs = rest[:-1]
    xs = rest[-1]
    half = own_ref.shape[3]
    for c in range(2):
        xs[c, :, 0:half] = own_ref[c, 0]
        xs[c, :, half:] = par_ref[c, 0]
    dims = (((1,), (1,)), ((), ()))
    table = tab_ref[...]
    from_real = lax.dot_general(table, xs[0], dims, preferred_element_type=jnp.float32)
    from_imag = lax.dot_general(table, xs[1], dims, preferred_element_type=jnp.float32)
    bins = table.shape[0] // 2
    scale = 1.0 / math.sqrt(F)
    real = ((from_real[:bins] - from_imag[bins:]) * scale).astype(jnp.bfloat16)
    imag = ((from_real[bins:] + from_imag[:bins]) * scale).astype(jnp.bfloat16)
    early = outs[-1]
    pieces = len(outs) - 1
    size = bins // pieces
    late = outs[0].shape[2]
    for s in range(pieces):
        for c, part in enumerate((real, imag)):
            outs[s][c, 0] = part[s * size : s * size + late]
            early[c, 0, s] = part[s * size + late : (s + 1) * size]


def range_transform(own, partner, table, pieces, early):
    _, cuts, cols, half = own.shape
    late = table.shape[0] // 2 // pieces - early
    spec = pl.BlockSpec((2, 1, cols, half), lambda i: (0, i, 0, 0))
    return pl.pallas_call(
        range_body,
        out_shape=[jax.ShapeDtypeStruct((2, cuts, late, cols), jnp.bfloat16)] * pieces
        + [jax.ShapeDtypeStruct((2, cuts, pieces, early, cols), jnp.bfloat16)],
        grid=(cuts,),
        in_specs=[spec, spec, pl.BlockSpec(table.shape, lambda i: (0, 0))],
        out_specs=[pl.BlockSpec((2, 1, late, cols), lambda i: (0, i, 0, 0))] * pieces
        + [pl.BlockSpec((2, 1, pieces, early, cols), lambda i: (0, i, 0, 0, 0))],
        scratch_shapes=[pltpu.VMEM((2, cols, 2 * half), jnp.bfloat16)],
        compiler_params=params(),
        cost_estimate=cost(4 * table.size * cuts * cols, 6 * 10**6),
        name="range_dft",
    )(own, partner, table)


def cross_body(pieces, *refs):
    cos_ref, sin_ref = refs[pieces : pieces + 2]
    out_ref, lhs = refs[-2:]
    _, cuts, bins, cols = refs[0].shape

    @pl.when(pl.program_id(0) == 0)
    def _():
        for s in range(pieces):
            block = refs[s][...].reshape(2 * cuts * bins, cols)
            lhs[:, s * cols : (s + 1) * cols] = block

    left = lhs[...]
    by_cos = jnp.dot(left, cos_ref[...], preferred_element_type=jnp.float32)
    by_sin = jnp.dot(left, sin_ref[...], preferred_element_type=jnp.float32)
    rows = cuts * bins
    scale = 1.0 / math.sqrt(A)
    shape = (cuts, bins, cos_ref.shape[1])
    real = (by_cos[:rows] - by_sin[rows:]) * scale
    imag = (by_sin[:rows] + by_cos[rows:]) * scale
    out_ref[0] = real.astype(jnp.bfloat16).reshape(shape)
    out_ref[1] = imag.astype(jnp.bfloat16).reshape(shape)


def cross_transform(pieces, cos_a, sin_a, image=None, total=None, at=0):
    _, cuts, bins, cols = pieces[0].shape
    depth, width = cos_a.shape
    tile = 256
    whole = pl.BlockSpec((2, cuts, bins, cols), lambda i: (0, 0, 0, 0))
    table = pl.BlockSpec((depth, tile), lambda i: (0, i))
    count = len(pieces)
    held = [] if image is None else [image]
    return pl.pallas_call(
        functools.partial(cross_body, count),
        out_shape=jax.ShapeDtypeStruct((2, cuts, total or bins, width), jnp.bfloat16),
        grid=(width // tile,),
        in_specs=[whole] * count + [table, table] + [pl.BlockSpec(memory_space=pl.ANY)] * len(held),
        out_specs=pl.BlockSpec((2, cuts, bins, tile), lambda i: (0, 0, at // bins, i)),
        scratch_shapes=[pltpu.VMEM((2 * cuts * bins, depth), jnp.bfloat16)],
        input_output_aliases={count + 2: 0} if held else {},
        compiler_params=params(),
        cost_estimate=cost(8 * cuts * bins * depth * width, 8 * 10**6),
        name="cross_dft",
    )(*pieces, cos_a, sin_a, *held)


def height_body(count, *refs):
    tab_ref = refs[count]
    out_ref, data = refs[-2:]
    at = 0
    for ref in refs[:count]:
        parts, cuts, rows, width = ref.shape
        size = parts * cuts * rows
        data[at : at + size, :] = ref[...].reshape(size, width)
        at += size
    parts, heights, rows, width = out_ref.shape
    scale = 1.0 / math.sqrt(E)
    tile = 256
    for t in range(width // tile):
        cols = slice(t * tile, (t + 1) * tile)
        total = jnp.dot(tab_ref[...], data[:, cols], preferred_element_type=jnp.float32)
        total = (total * scale).astype(jnp.bfloat16)
        out_ref[:, :, :, cols] = total.reshape(parts, heights, rows, tile)


def height_transform(chunks, table, image):
    _, heights, _, width = image.shape
    bins = chunks[0].shape[2]
    count = len(chunks)
    specs = [
        pl.BlockSpec((2, x.shape[1], GROUP, width), lambda i: (0, 0, i, 0)) for x in chunks
    ]
    return pl.pallas_call(
        functools.partial(height_body, count),
        out_shape=jax.ShapeDtypeStruct(image.shape, jnp.bfloat16),
        grid=(bins // GROUP,),
        in_specs=specs
        + [pl.BlockSpec(table.shape, lambda i: (0, 0)), pl.BlockSpec(memory_space=pl.ANY)],
        out_specs=pl.BlockSpec((2, heights, GROUP, width), lambda i: (0, 0, i, 0)),
        scratch_shapes=[pltpu.VMEM((table.shape[1], width), jnp.bfloat16)],
        input_output_aliases={count + 1: 0},
        compiler_params=params(),
        cost_estimate=cost(2 * table.size * width * (bins // GROUP), 2 * 10**7),
        name="height_dft",
    )(*chunks, table, image)


def early_body(count, *refs):
    tab_ref = refs[count]
    outs = refs[count + 1 : -1]
    data = refs[-1]
    scale = 1.0 / math.sqrt(E)
    for s, out_ref in enumerate(outs):
        at = 0
        for ref in refs[:count]:
            parts, cuts, _, rows, width = ref.shape
            size = parts * cuts * rows
            data[s, at : at + size, :] = ref[:, :, s].reshape(size, width)
            at += size
        total = jnp.dot(tab_ref[...], data[s], preferred_element_type=jnp.float32)
        out_ref[...] = (total * scale).astype(jnp.bfloat16).reshape(out_ref.shape)


def early_heights(chunks, table, heights, group):
    _, _, pieces, _, cols = chunks[0].shape
    count = len(chunks)
    specs = [
        pl.BlockSpec((2, x.shape[1], pieces, GROUP, cols), lambda i: (0, 0, 0, group, 0))
        for x in chunks
    ]
    out = (2, heights, GROUP, cols)
    return pl.pallas_call(
        functools.partial(early_body, count),
        out_shape=[jax.ShapeDtypeStruct(out, jnp.bfloat16)] * pieces,
        grid=(1,),
        in_specs=specs + [pl.BlockSpec(table.shape, lambda i: (0, 0))],
        out_specs=[pl.BlockSpec(out, lambda i: (0, 0, 0, 0))] * pieces,
        scratch_shapes=[pltpu.VMEM((pieces, table.shape[1], cols), jnp.bfloat16)],
        compiler_params=params(),
        cost_estimate=cost(2 * table.size * cols * pieces, 4 * 10**6),
        name="early_height",
    )(*chunks, table)


def height_table(height_ids, elev_starts, e_here):
    columns = []
    for start in elev_starts:
        first = 0
        for cuts in CUTS:
            ids = start + first + jnp.arange(cuts, dtype=jnp.int32)
            cos_e, sin_e = table_pair(height_ids, ids, E)
            columns.append(jnp.concatenate([cos_e, sin_e]))
            columns.append(jnp.concatenate([-sin_e, cos_e]))
            first += cuts
    small = jnp.concatenate(columns, axis=1)
    rows, cols = small.shape
    row = jnp.arange(rows * GROUP, dtype=jnp.int32)
    col = jnp.arange(cols * GROUP, dtype=jnp.int32)
    take_row = (row[:, None] // GROUP == jnp.arange(rows)[None]).astype(jnp.bfloat16)
    take_col = (jnp.arange(cols)[:, None] == col[None] // GROUP).astype(jnp.bfloat16)
    wide = jnp.dot(jnp.dot(take_row, small), take_col)
    same = row[:, None] % GROUP == col[None] % GROUP
    return jnp.where(same, wide, jnp.zeros((), jnp.bfloat16))


def ring(pieces, axis):
    count = len(pieces)
    return [pieces[0]] + [
        lax.ppermute(pieces[s], axis, [(i, (i + s) % count) for i in range(count)])
        for s in range(1, count)
    ]


def pipelined(polar, band_offset, tap_count, tap_weight):
    _, e_here, col_count, freq_count = polar.shape
    az_count = lax.axis_size("az")
    fq_count = lax.axis_size("fq")
    el_count = lax.axis_size("el")
    az, fq, el = (lax.axis_index(name) for name in ("az", "fq", "el"))
    bins = F // (fq_count * az_count)
    heights = E // el_count
    early = EARLY * GROUP
    late = bins - early
    ends = az_count - 1
    left = lax.ppermute(
        polar[:, :, col_count - HW :], "az", [(i, i + 1) for i in range(ends)]
    )
    right = lax.ppermute(polar[:, :, :HW], "az", [(i + 1, i) for i in range(ends)])
    weights = band_weights(band_offset, tap_count, tap_weight)

    shifts = jnp.arange(az_count, dtype=jnp.int32)
    targets = (az + shifts) % az_count
    local = jnp.arange(bins, dtype=jnp.int32)
    range_ids = ((targets[:, None] * fq_count + fq) * bins + local[None]).reshape(-1)
    f_local = jnp.arange(freq_count, dtype=jnp.int32)
    freq_ids = jnp.concatenate([fq * freq_count + f_local, (1 - fq) * freq_count + f_local])
    cos_f, sin_f = trig_pair(range_ids, freq_ids, F)
    range_table = jnp.concatenate([cos_f, sin_f])

    sources = (az - shifts) % az_count
    col_local = jnp.arange(col_count, dtype=jnp.int32)
    azim_ids = (sources[:, None] * col_count + col_local[None]).reshape(-1)
    cos_a, sin_a = trig_pair(azim_ids, jnp.arange(A, dtype=jnp.int32), A)

    height_ids = el * heights + jnp.arange(heights, dtype=jnp.int32)
    elev_starts = [(el - s) % el_count * e_here for s in range(el_count)]
    table = height_table(height_ids, elev_starts, e_here)

    firsts = [sum(CUTS[:c]) for c in range(len(CUTS))]
    mixed = []
    pieces = []
    ahead = [[] for _ in range(el_count)]
    for chunk, cuts in enumerate(CUTS):
        gate = weights
        if chunk >= 2:
            gate, _ = lax.optimization_barrier((weights, pieces[chunk - 2][0]))
        mixed.append(interpolate(polar, left, right, gate, firsts[chunk], cuts))
        if chunk >= 1:
            advance(chunk - 1, mixed, range_table, early, pieces, ahead, el_count, az_count)
    advance(len(CUTS) - 1, mixed, range_table, early, pieces, ahead, el_count, az_count)

    passed = [[] for _ in range(el_count)]
    for chunk in range(len(CUTS)):
        crossed = cross_transform(ring(pieces[chunk], "az"), cos_a, sin_a)
        for s, block in enumerate(ring([crossed] * el_count, "el")):
            passed[s].append(block)

    image = None
    for group in range(EARLY):
        blocks = early_heights(sum(ahead, []), table, heights, group)
        image = cross_transform(
            ring(blocks, "az"), cos_a, sin_a, image, bins, late + group * GROUP
        )
    return height_transform(sum(passed, []), table, image)


def advance(chunk, mixed, range_table, early, pieces, ahead, el_count, az_count):
    partner = lax.ppermute(mixed[chunk], "fq", [(0, 1), (1, 0)])
    outs = range_transform(mixed[chunk], partner, range_table, az_count, early)
    pieces.append(outs[:-1])
    for s, block in enumerate(ring([outs[-1]] * el_count, "el")):
        ahead[s].append(block)


def pick(polar, band_offset, tap_count, tap_weight):
    _, e_here, col_count, freq_count = polar.shape
    bins = F // (lax.axis_size("fq") * lax.axis_size("az"))
    fits = (
        lax.axis_size("fq") == 2
        and lax.axis_size("az") <= 4
        and e_here == sum(CUTS)
        and bins % GROUP == 0
        and bins > EARLY * GROUP
        and col_count % LANES == 0
        and freq_count % LANES == 0
    )
    plan = pipelined if fits else on_device
    return plan(polar, band_offset, tap_count, tap_weight)


def solution(mesh):
    in_specs = (
        P(None, ("grp", "el"), "az", "fq"),
        P("az", "fq"),
        P("az", "fq"),
        P(None, "az", "fq"),
    )
    out_specs = P(None, ("grp", "el"), ("az", "fq"), None)
    return jax.shard_map(
        pick, mesh=mesh, in_specs=in_specs, out_specs=out_specs, check_vma=False
    )
```

```python
import functools
import math

import jax
import jax.numpy as jnp
from jax import lax
from jax.experimental import pallas as pl
from jax.experimental.pallas import tpu as pltpu
from jax.sharding import PartitionSpec as P


F = 768
A = 1024
E = 32
HW = 8
KT = 8
LANES = 128
GROUP = 16
CUTS = (2, 2, 4, 4, 4)
EARLY = 2


def with_halo(cells, sides, width):
    for axis, dim in sides:
        count = lax.axis_size(axis)
        ends = count - 1
        head = lax.slice_in_dim(cells, 0, width, axis=dim)
        tail = lax.slice_in_dim(cells, cells.shape[dim] - width, cells.shape[dim], axis=dim)
        cells = jnp.concatenate(
            [
                lax.ppermute(tail, axis, [(i, (i + 1) % count) for i in range(ends)]),
                cells,
                lax.ppermute(head, axis, [((i + 1) % count, i) for i in range(ends)]),
            ],
            axis=dim,
        )
    return cells


def table_pair(row_ids, col_ids, length):
    product = row_ids[:, None] * col_ids[None, :] % length
    angle = product.astype(jnp.float32) * (2.0 * math.pi / length)
    return (jnp.cos(angle).astype(jnp.bfloat16), jnp.sin(angle).astype(jnp.bfloat16))


def on_device(polar, band_offset, tap_count, tap_weight):
    shape_all = polar.shape
    col_count = shape_all[2]
    freq_count = shape_all[3]
    az_count = lax.axis_size("az")
    fq_count = lax.axis_size("fq")
    el_count = lax.axis_size("el")
    padded = with_halo(polar, (("az", 2),), HW)
    window = col_count + 2 * HW
    column = jnp.arange(col_count, dtype=jnp.int32)[:, None]
    position = jnp.arange(window, dtype=jnp.int32)[None, :, None]
    band_matrix = jnp.zeros((col_count, window, freq_count), jnp.bfloat16)
    for tap_index in range(KT):
        reach = column + HW + band_offset + tap_index
        matches = (position == reach[:, None, :]) & (tap_index < tap_count)[:, None, :]
        band_matrix = jnp.where(matches, tap_weight[tap_index][:, None, :], band_matrix)
    interpolated = jnp.einsum(
        "jaf,ceaf->cejf", band_matrix, padded, preferred_element_type=jnp.float32
    ).astype(jnp.bfloat16)
    fq_index = lax.axis_index("fq")
    bin_count = F // (fq_count * az_count)
    az_block = jnp.arange(az_count, dtype=jnp.int32)[:, None]
    bin_local = jnp.arange(bin_count, dtype=jnp.int32)[None, :]
    range_bins = ((az_block * fq_count + fq_index) * bin_count + bin_local).reshape(-1)
    cos_f, sin_f = table_pair(jnp.arange(F, dtype=jnp.int32), range_bins, F)
    shard_piece = lax.all_gather(interpolated, "fq", axis=3, tiled=True)
    cos_rows = cos_f
    sin_rows = sin_f
    real_part = jnp.einsum(
        "ejf,fk->ekj", shard_piece[0], cos_rows, preferred_element_type=jnp.float32
    ) - jnp.einsum("ejf,fk->ekj", shard_piece[1], sin_rows, preferred_element_type=jnp.float32)
    imag_part = jnp.einsum(
        "ejf,fk->ekj", shard_piece[0], sin_rows, preferred_element_type=jnp.float32
    ) + jnp.einsum("ejf,fk->ekj", shard_piece[1], cos_rows, preferred_element_type=jnp.float32)
    summed = jnp.stack([real_part, imag_part])
    ranged = (summed * (1.0 / math.sqrt(F))).astype(jnp.bfloat16)
    azim_ids = jnp.arange(A, dtype=jnp.int32)
    cos_a, sin_a = table_pair(azim_ids, azim_ids, A)
    block_data = lax.all_to_all(ranged, "az", split_axis=2, concat_axis=3, tiled=True)
    real_part = jnp.einsum(
        "ekj,jm->ekm", block_data[0], cos_a, preferred_element_type=jnp.float32
    ) - jnp.einsum("ekj,jm->ekm", block_data[1], sin_a, preferred_element_type=jnp.float32)
    imag_part = jnp.einsum(
        "ekj,jm->ekm", block_data[0], sin_a, preferred_element_type=jnp.float32
    ) + jnp.einsum("ekj,jm->ekm", block_data[1], cos_a, preferred_element_type=jnp.float32)
    crossed = (jnp.stack([real_part, imag_part]) * (1.0 / math.sqrt(A))).astype(jnp.bfloat16)
    elev_ids = jnp.arange(E, dtype=jnp.int32)
    el_index = lax.axis_index("el")
    height_count = E // el_count
    height_rows = el_index * height_count + jnp.arange(height_count, dtype=jnp.int32)
    cos_e, sin_e = table_pair(elev_ids, height_rows, E)
    shard_piece = lax.all_gather(crossed, "el", axis=1, tiled=True)
    cos_rows = cos_e
    sin_rows = sin_e
    real_part = jnp.einsum(
        "eh,ekm->hkm", cos_rows, shard_piece[0], preferred_element_type=jnp.float32
    ) - jnp.einsum("eh,ekm->hkm", sin_rows, shard_piece[1], preferred_element_type=jnp.float32)
    imag_part = jnp.einsum(
        "eh,ekm->hkm", sin_rows, shard_piece[0], preferred_element_type=jnp.float32
    ) + jnp.einsum("eh,ekm->hkm", cos_rows, shard_piece[1], preferred_element_type=jnp.float32)
    totals = jnp.stack([real_part, imag_part])
    image_out = (totals * (1.0 / math.sqrt(E))).astype(jnp.bfloat16)
    return image_out


def trig_pair(row_ids, col_ids, length, split=32):
    fine = jnp.arange(split, dtype=jnp.int32)

    def small(factor):
        product = (factor[:, None] * col_ids[None, :]) % length
        angle = product.astype(jnp.float32) * (2.0 * math.pi / length)
        return jnp.cos(angle), jnp.sin(angle)

    block = row_ids.shape[0] // split
    starts = row_ids.reshape(block, split)[:, 0]
    low_cos, low_sin = small(fine)
    high_cos, high_sin = small(starts)
    low_cos, low_sin, high_cos, high_sin = lax.optimization_barrier(
        (low_cos, low_sin, high_cos, high_sin)
    )
    shape = (block * split, col_ids.shape[0])
    cos_t = high_cos[:, None] * low_cos[None] - high_sin[:, None] * low_sin[None]
    sin_t = high_sin[:, None] * low_cos[None] + high_cos[:, None] * low_sin[None]
    return (
        cos_t.reshape(shape).astype(jnp.bfloat16),
        sin_t.reshape(shape).astype(jnp.bfloat16),
    )


def cost(flops, moved):
    return pl.CostEstimate(flops=int(flops), bytes_accessed=int(moved), transcendentals=0)


def params():
    return pltpu.CompilerParams(vmem_limit_bytes=48 * 1024 * 1024)


def weights_body(off_ref, cnt_ref, tap_ref, w_ref):
    rows = 16

    @pl.loop(0, off_ref.shape[0] // rows)
    def _(step):
        at = pl.ds(pl.multiple_of(step * rows, rows), rows)
        off = off_ref[at, :]
        cnt = cnt_ref[at, :]
        taps = [
            jnp.where(t < cnt, tap_ref[t, at, :].astype(jnp.float32), 0.0) for t in range(KT)
        ]
        for d in range(2 * HW + 1):
            rel = (d - HW) - off
            acc = jnp.zeros(off.shape, jnp.float32)
            for t in range(KT):
                acc = jnp.where(rel == t, taps[t], acc)
            w_ref[d, at, :] = acc.astype(jnp.bfloat16)


def band_weights(band_offset, tap_count, tap_weight):
    cols, freqs = band_offset.shape
    taps = 2 * HW + 1
    return pl.pallas_call(
        weights_body,
        out_shape=jax.ShapeDtypeStruct((taps, cols, freqs), jnp.bfloat16),
        grid=(freqs // LANES,),
        in_specs=[
            pl.BlockSpec((cols, LANES), lambda i: (0, i)),
            pl.BlockSpec((cols, LANES), lambda i: (0, i)),
            pl.BlockSpec((KT, cols, LANES), lambda i: (0, 0, i)),
        ],
        out_specs=pl.BlockSpec((taps, cols, LANES), lambda i: (0, 0, i)),
        compiler_params=params(),
        cost_estimate=cost(10**9, 6 * 10**6),
        name="weights",
    )(band_offset, tap_count, tap_weight)


def interp_body(x_ref, l_ref, r_ref, w_ref, o_ref, buf):
    cuts = x_ref.shape[1]
    cols = x_ref.shape[2]
    rows = 16
    for c in range(2):
        for e in range(cuts):
            p = c * cuts + e
            buf[p, 0:HW, :] = l_ref[c, e].astype(jnp.float32)
            buf[p, HW : HW + cols, :] = x_ref[c, e].astype(jnp.float32)
            buf[p, HW + cols : 2 * HW + cols, :] = r_ref[c, e].astype(jnp.float32)

    @pl.loop(0, cols // rows)
    def _(step):
        base = pl.multiple_of(step * rows, rows)
        weights = [
            w_ref[d, pl.ds(base, rows), :].astype(jnp.float32) for d in range(2 * HW + 1)
        ]
        for c in range(2):
            for e in range(cuts):
                p = c * cuts + e
                acc = weights[0] * buf[p, pl.ds(base, rows), :]
                for d in range(1, 2 * HW + 1):
                    acc = acc + weights[d] * buf[p, pl.ds(base + d, rows), :]
                o_ref[c, e, pl.ds(base, rows), :] = acc.astype(jnp.bfloat16)


def interpolate(polar, left, right, weights, first, cuts):
    _, _, cols, freqs = polar.shape
    taps = 2 * HW + 1
    chunk = first // cuts
    return pl.pallas_call(
        interp_body,
        out_shape=jax.ShapeDtypeStruct((2, cuts, cols, freqs), jnp.bfloat16),
        grid=(freqs // LANES,),
        in_specs=[
            pl.BlockSpec((2, cuts, cols, LANES), lambda i: (0, chunk, 0, i)),
            pl.BlockSpec((2, cuts, HW, LANES), lambda i: (0, chunk, 0, i)),
            pl.BlockSpec((2, cuts, HW, LANES), lambda i: (0, chunk, 0, i)),
            pl.BlockSpec((taps, cols, LANES), lambda i: (0, 0, i)),
        ],
        out_specs=pl.BlockSpec((2, cuts, cols, LANES), lambda i: (0, 0, 0, i)),
        scratch_shapes=[pltpu.VMEM((2 * cuts, cols + 2 * HW, LANES), jnp.float32)],
        compiler_params=params(),
        cost_estimate=cost(10**9, 6 * 10**6),
        name="interp",
    )(polar, left, right, weights)


def range_body(own_ref, par_ref, tab_ref, *rest):
    outs = rest[:-1]
    xs = rest[-1]
    half = own_ref.shape[3]
    for c in range(2):
        xs[c, :, 0:half] = own_ref[c, 0]
        xs[c, :, half:] = par_ref[c, 0]
    dims = (((1,), (1,)), ((), ()))
    table = tab_ref[...]
    from_real = lax.dot_general(table, xs[0], dims, preferred_element_type=jnp.float32)
    from_imag = lax.dot_general(table, xs[1], dims, preferred_element_type=jnp.float32)
    bins = table.shape[0] // 2
    scale = 1.0 / math.sqrt(F)
    real = ((from_real[:bins] - from_imag[bins:]) * scale).astype(jnp.bfloat16)
    imag = ((from_real[bins:] + from_imag[:bins]) * scale).astype(jnp.bfloat16)
    early = outs[-1]
    pieces = len(outs) - 1
    size = bins // pieces
    late = outs[0].shape[2]
    for s in range(pieces):
        for c, part in enumerate((real, imag)):
            outs[s][c, 0] = part[s * size : s * size + late]
            early[c, 0, s] = part[s * size + late : (s + 1) * size]


def range_transform(own, partner, table, pieces, early):
    _, cuts, cols, half = own.shape
    late = table.shape[0] // 2 // pieces - early
    spec = pl.BlockSpec((2, 1, cols, half), lambda i: (0, i, 0, 0))
    return pl.pallas_call(
        range_body,
        out_shape=[jax.ShapeDtypeStruct((2, cuts, late, cols), jnp.bfloat16)] * pieces
        + [jax.ShapeDtypeStruct((2, cuts, pieces, early, cols), jnp.bfloat16)],
        grid=(cuts,),
        in_specs=[spec, spec, pl.BlockSpec(table.shape, lambda i: (0, 0))],
        out_specs=[pl.BlockSpec((2, 1, late, cols), lambda i: (0, i, 0, 0))] * pieces
        + [pl.BlockSpec((2, 1, pieces, early, cols), lambda i: (0, i, 0, 0, 0))],
        scratch_shapes=[pltpu.VMEM((2, cols, 2 * half), jnp.bfloat16)],
        compiler_params=params(),
        cost_estimate=cost(4 * table.size * cuts * cols, 6 * 10**6),
        name="range_dft",
    )(own, partner, table)


def cross_body(pieces, *refs):
    cos_ref, sin_ref = refs[pieces : pieces + 2]
    out_ref, lhs = refs[-2:]
    _, cuts, bins, cols = refs[0].shape

    @pl.when(pl.program_id(0) == 0)
    def _():
        for s in range(pieces):
            block = refs[s][...].reshape(2 * cuts * bins, cols)
            lhs[:, s * cols : (s + 1) * cols] = block

    left = lhs[...]
    by_cos = jnp.dot(left, cos_ref[...], preferred_element_type=jnp.float32)
    by_sin = jnp.dot(left, sin_ref[...], preferred_element_type=jnp.float32)
    rows = cuts * bins
    scale = 1.0 / math.sqrt(A)
    shape = (cuts, bins, cos_ref.shape[1])
    real = (by_cos[:rows] - by_sin[rows:]) * scale
    imag = (by_sin[:rows] + by_cos[rows:]) * scale
    out_ref[0] = real.astype(jnp.bfloat16).reshape(shape)
    out_ref[1] = imag.astype(jnp.bfloat16).reshape(shape)


def cross_transform(pieces, cos_a, sin_a, image=None, total=None, at=0):
    _, cuts, bins, cols = pieces[0].shape
    depth, width = cos_a.shape
    tile = 256
    whole = pl.BlockSpec((2, cuts, bins, cols), lambda i: (0, 0, 0, 0))
    table = pl.BlockSpec((depth, tile), lambda i: (0, i))
    count = len(pieces)
    held = [] if image is None else [image]
    return pl.pallas_call(
        functools.partial(cross_body, count),
        out_shape=jax.ShapeDtypeStruct((2, cuts, total or bins, width), jnp.bfloat16),
        grid=(width // tile,),
        in_specs=[whole] * count + [table, table] + [pl.BlockSpec(memory_space=pl.ANY)] * len(held),
        out_specs=pl.BlockSpec((2, cuts, bins, tile), lambda i: (0, 0, at // bins, i)),
        scratch_shapes=[pltpu.VMEM((2 * cuts * bins, depth), jnp.bfloat16)],
        input_output_aliases={count + 2: 0} if held else {},
        compiler_params=params(),
        cost_estimate=cost(8 * cuts * bins * depth * width, 8 * 10**6),
        name="cross_dft",
    )(*pieces, cos_a, sin_a, *held)


def height_body(count, *refs):
    tab_ref = refs[count]
    out_ref, data = refs[-2:]
    at = 0
    for ref in refs[:count]:
        parts, cuts, rows, width = ref.shape
        size = parts * cuts * rows
        data[at : at + size, :] = ref[...].reshape(size, width)
        at += size
    parts, heights, rows, width = out_ref.shape
    scale = 1.0 / math.sqrt(E)
    tile = 256
    for t in range(width // tile):
        cols = slice(t * tile, (t + 1) * tile)
        total = jnp.dot(tab_ref[...], data[:, cols], preferred_element_type=jnp.float32)
        total = (total * scale).astype(jnp.bfloat16)
        out_ref[:, :, :, cols] = total.reshape(parts, heights, rows, tile)


def height_transform(chunks, table, heights, total, bins):
    width = chunks[0].shape[3]
    count = len(chunks)
    specs = [
        pl.BlockSpec((2, x.shape[1], GROUP, width), lambda i: (0, 0, i, 0)) for x in chunks
    ]
    return pl.pallas_call(
        functools.partial(height_body, count),
        out_shape=jax.ShapeDtypeStruct((2, heights, total, width), jnp.bfloat16),
        grid=(bins // GROUP,),
        in_specs=specs + [pl.BlockSpec(table.shape, lambda i: (0, 0))],
        out_specs=pl.BlockSpec((2, heights, GROUP, width), lambda i: (0, 0, i, 0)),
        scratch_shapes=[pltpu.VMEM((table.shape[1], width), jnp.bfloat16)],
        compiler_params=params(),
        cost_estimate=cost(2 * table.size * width * (bins // GROUP), 2 * 10**7),
        name="height_dft",
    )(*chunks, table)


def early_body(count, *refs):
    tab_ref = refs[count]
    outs = refs[count + 1 : -1]
    data = refs[-1]
    scale = 1.0 / math.sqrt(E)
    for s, out_ref in enumerate(outs):
        at = 0
        for ref in refs[:count]:
            parts, cuts, _, rows, width = ref.shape
            size = parts * cuts * rows
            data[s, at : at + size, :] = ref[:, :, s].reshape(size, width)
            at += size
        total = jnp.dot(tab_ref[...], data[s], preferred_element_type=jnp.float32)
        out_ref[...] = (total * scale).astype(jnp.bfloat16).reshape(out_ref.shape)


def early_heights(chunks, table, heights, group):
    _, _, pieces, _, cols = chunks[0].shape
    count = len(chunks)
    specs = [
        pl.BlockSpec((2, x.shape[1], pieces, GROUP, cols), lambda i: (0, 0, 0, group, 0))
        for x in chunks
    ]
    out = (2, heights, GROUP, cols)
    return pl.pallas_call(
        functools.partial(early_body, count),
        out_shape=[jax.ShapeDtypeStruct(out, jnp.bfloat16)] * pieces,
        grid=(1,),
        in_specs=specs + [pl.BlockSpec(table.shape, lambda i: (0, 0))],
        out_specs=[pl.BlockSpec(out, lambda i: (0, 0, 0, 0))] * pieces,
        scratch_shapes=[pltpu.VMEM((pieces, table.shape[1], cols), jnp.bfloat16)],
        compiler_params=params(),
        cost_estimate=cost(2 * table.size * cols * pieces, 4 * 10**6),
        name="early_height",
    )(*chunks, table)


def height_table(height_ids, elev_starts):
    columns = []
    for start in elev_starts:
        first = 0
        for cuts in CUTS:
            ids = start + first + jnp.arange(cuts, dtype=jnp.int32)
            cos_e, sin_e = table_pair(height_ids, ids, E)
            columns.append(jnp.concatenate([cos_e, sin_e]))
            columns.append(jnp.concatenate([-sin_e, cos_e]))
            first += cuts
    small = jnp.concatenate(columns, axis=1)
    rows, cols = small.shape
    row = jnp.arange(rows * GROUP, dtype=jnp.int32)
    col = jnp.arange(cols * GROUP, dtype=jnp.int32)
    take_row = (row[:, None] // GROUP == jnp.arange(rows)[None]).astype(jnp.bfloat16)
    take_col = (jnp.arange(cols)[:, None] == col[None] // GROUP).astype(jnp.bfloat16)
    wide = jnp.dot(jnp.dot(take_row, small), take_col)
    same = row[:, None] % GROUP == col[None] % GROUP
    return jnp.where(same, wide, jnp.zeros((), jnp.bfloat16))


def ring(pieces, axis):
    count = len(pieces)
    out = [pieces[0]]
    for s in range(1, count):
        out.append(
            lax.ppermute(pieces[s], axis, [(i, (i + s) % count) for i in range(count)])
        )
    return out


def kernel_order():
    count = len(CUTS)
    order = [("interp", 0)]
    for chunk in range(1, count):
        order += [("interp", chunk), ("range", chunk - 1)]
    order += [("range", count - 1)]
    order += [("cross", chunk) for chunk in range(count - 1)]
    order += [("early", group) for group in range(EARLY)]
    order += [("cross", count - 1), ("height", 0)]
    order += [("last", group) for group in range(EARLY)]
    return order


def pipelined(polar, band_offset, tap_count, tap_weight):
    _, e_here, col_count, freq_count = polar.shape
    az_count = lax.axis_size("az")
    fq_count = lax.axis_size("fq")
    el_count = lax.axis_size("el")
    az, fq, el = (lax.axis_index(name) for name in ("az", "fq", "el"))
    bins = F // (fq_count * az_count)
    heights = E // el_count
    early = EARLY * GROUP
    late = bins - early
    ends = az_count - 1
    left = lax.ppermute(
        polar[:, :, col_count - HW :], "az", [(i, i + 1) for i in range(ends)]
    )
    right = lax.ppermute(polar[:, :, :HW], "az", [(i + 1, i) for i in range(ends)])
    weights = band_weights(band_offset, tap_count, tap_weight)

    shifts = jnp.arange(az_count, dtype=jnp.int32)
    targets = (az + shifts) % az_count
    local = jnp.arange(bins, dtype=jnp.int32)
    range_ids = ((targets[:, None] * fq_count + fq) * bins + local[None]).reshape(-1)
    f_local = jnp.arange(freq_count, dtype=jnp.int32)
    freq_ids = jnp.concatenate([fq * freq_count + f_local, (1 - fq) * freq_count + f_local])
    cos_f, sin_f = trig_pair(range_ids, freq_ids, F)
    range_table = jnp.concatenate([cos_f, sin_f])

    sources = (az - shifts) % az_count
    col_local = jnp.arange(col_count, dtype=jnp.int32)
    azim_ids = (sources[:, None] * col_count + col_local[None]).reshape(-1)
    cos_a, sin_a = trig_pair(azim_ids, jnp.arange(A, dtype=jnp.int32), A)

    height_ids = el * heights + jnp.arange(heights, dtype=jnp.int32)
    elev_starts = [(el - s) % el_count * e_here for s in range(el_count)]
    table = height_table(height_ids, elev_starts)

    firsts = [sum(CUTS[:c]) for c in range(len(CUTS))]
    mixed, pieces, partners = {}, {}, {}
    ahead = [[] for _ in range(el_count)]
    passed = [[] for _ in range(el_count)]
    early_blocks = {}
    last = None

    for kind, n in kernel_order():
        if kind == "interp":
            gate = hold(weights, last)
            last = interpolate(polar, left, right, gate, firsts[n], CUTS[n])
            mixed[n] = last
        elif kind == "range":
            gate = hold(range_table, last)
            outs = range_transform(mixed[n], partners[n], gate, az_count, early)
            last = outs[0]
        elif kind == "cross":
            own = [hold(pieces[n][0], last)] + pieces[n][1:]
            last = cross_transform(own, cos_a, sin_a)
        elif kind == "early":
            blocks = early_heights(sum(ahead, []), hold(table, last), heights, n)
            last = blocks[0]
        elif kind == "height":
            gate = hold(table, last)
            image = height_transform(sum(passed, []), gate, heights, bins, late)
        else:
            image = cross_transform(early_blocks[n], cos_a, sin_a, image, bins, late + n * GROUP)
        if kind == "interp":
            partners[n] = ring([last, last], "fq")[1]
        elif kind == "range":
            pieces[n] = ring(outs[:-1], "az")
            for s, block in enumerate(ring([outs[-1]] * el_count, "el")):
                ahead[s].append(block)
        elif kind == "cross":
            for s, block in enumerate(ring([last] * el_count, "el")):
                passed[s].append(block)
        elif kind == "early":
            early_blocks[n] = ring(blocks, "az")
    return image


def hold(value, last):
    return value if last is None else lax.optimization_barrier((value, last))[0]


def pick(polar, band_offset, tap_count, tap_weight):
    _, e_here, col_count, freq_count = polar.shape
    bins = F // (lax.axis_size("fq") * lax.axis_size("az"))
    fits = (
        lax.axis_size("fq") == 2
        and lax.axis_size("az") <= 4
        and e_here == sum(CUTS)
        and bins % GROUP == 0
        and bins > EARLY * GROUP
        and col_count % LANES == 0
        and freq_count % LANES == 0
    )
    if not fits:
        return on_device(polar, band_offset, tap_count, tap_weight)
    return pipelined(polar, band_offset, tap_count, tap_weight)


def solution(mesh):
    in_specs = (
        P(None, ("grp", "el"), "az", "fq"),
        P("az", "fq"),
        P("az", "fq"),
        P(None, "az", "fq"),
    )
    out_specs = P(None, ("grp", "el"), ("az", "fq"), None)
    return jax.shard_map(
        pick, mesh=mesh, in_specs=in_specs, out_specs=out_specs, check_vma=False
    )
```

```python
import functools
import math

import jax
import jax.numpy as jnp
from jax import lax
from jax.experimental import pallas as pl
from jax.experimental.pallas import tpu as pltpu
from jax.sharding import PartitionSpec as P


F = 768
A = 1024
E = 32
HW = 8
KT = 8
LANES = 128
GROUP = 16
CUTS = (4, 4, 4, 4)
EARLY = 3
BEFORE = 2


def with_halo(cells, sides, width):
    for axis, dim in sides:
        count = lax.axis_size(axis)
        ends = count - 1
        head = lax.slice_in_dim(cells, 0, width, axis=dim)
        tail = lax.slice_in_dim(cells, cells.shape[dim] - width, cells.shape[dim], axis=dim)
        cells = jnp.concatenate(
            [
                lax.ppermute(tail, axis, [(i, (i + 1) % count) for i in range(ends)]),
                cells,
                lax.ppermute(head, axis, [((i + 1) % count, i) for i in range(ends)]),
            ],
            axis=dim,
        )
    return cells


def table_pair(row_ids, col_ids, length):
    product = row_ids[:, None] * col_ids[None, :] % length
    angle = product.astype(jnp.float32) * (2.0 * math.pi / length)
    return (jnp.cos(angle).astype(jnp.bfloat16), jnp.sin(angle).astype(jnp.bfloat16))


def on_device(polar, band_offset, tap_count, tap_weight):
    shape_all = polar.shape
    col_count = shape_all[2]
    freq_count = shape_all[3]
    az_count = lax.axis_size("az")
    fq_count = lax.axis_size("fq")
    el_count = lax.axis_size("el")
    padded = with_halo(polar, (("az", 2),), HW)
    window = col_count + 2 * HW
    column = jnp.arange(col_count, dtype=jnp.int32)[:, None]
    position = jnp.arange(window, dtype=jnp.int32)[None, :, None]
    band_matrix = jnp.zeros((col_count, window, freq_count), jnp.bfloat16)
    for tap_index in range(KT):
        reach = column + HW + band_offset + tap_index
        matches = (position == reach[:, None, :]) & (tap_index < tap_count)[:, None, :]
        band_matrix = jnp.where(matches, tap_weight[tap_index][:, None, :], band_matrix)
    interpolated = jnp.einsum(
        "jaf,ceaf->cejf", band_matrix, padded, preferred_element_type=jnp.float32
    ).astype(jnp.bfloat16)
    fq_index = lax.axis_index("fq")
    bin_count = F // (fq_count * az_count)
    az_block = jnp.arange(az_count, dtype=jnp.int32)[:, None]
    bin_local = jnp.arange(bin_count, dtype=jnp.int32)[None, :]
    range_bins = ((az_block * fq_count + fq_index) * bin_count + bin_local).reshape(-1)
    cos_f, sin_f = table_pair(jnp.arange(F, dtype=jnp.int32), range_bins, F)
    shard_piece = lax.all_gather(interpolated, "fq", axis=3, tiled=True)
    cos_rows = cos_f
    sin_rows = sin_f
    real_part = jnp.einsum(
        "ejf,fk->ekj", shard_piece[0], cos_rows, preferred_element_type=jnp.float32
    ) - jnp.einsum("ejf,fk->ekj", shard_piece[1], sin_rows, preferred_element_type=jnp.float32)
    imag_part = jnp.einsum(
        "ejf,fk->ekj", shard_piece[0], sin_rows, preferred_element_type=jnp.float32
    ) + jnp.einsum("ejf,fk->ekj", shard_piece[1], cos_rows, preferred_element_type=jnp.float32)
    summed = jnp.stack([real_part, imag_part])
    ranged = (summed * (1.0 / math.sqrt(F))).astype(jnp.bfloat16)
    azim_ids = jnp.arange(A, dtype=jnp.int32)
    cos_a, sin_a = table_pair(azim_ids, azim_ids, A)
    block_data = lax.all_to_all(ranged, "az", split_axis=2, concat_axis=3, tiled=True)
    real_part = jnp.einsum(
        "ekj,jm->ekm", block_data[0], cos_a, preferred_element_type=jnp.float32
    ) - jnp.einsum("ekj,jm->ekm", block_data[1], sin_a, preferred_element_type=jnp.float32)
    imag_part = jnp.einsum(
        "ekj,jm->ekm", block_data[0], sin_a, preferred_element_type=jnp.float32
    ) + jnp.einsum("ekj,jm->ekm", block_data[1], cos_a, preferred_element_type=jnp.float32)
    crossed = (jnp.stack([real_part, imag_part]) * (1.0 / math.sqrt(A))).astype(jnp.bfloat16)
    elev_ids = jnp.arange(E, dtype=jnp.int32)
    el_index = lax.axis_index("el")
    height_count = E // el_count
    height_rows = el_index * height_count + jnp.arange(height_count, dtype=jnp.int32)
    cos_e, sin_e = table_pair(elev_ids, height_rows, E)
    shard_piece = lax.all_gather(crossed, "el", axis=1, tiled=True)
    cos_rows = cos_e
    sin_rows = sin_e
    real_part = jnp.einsum(
        "eh,ekm->hkm", cos_rows, shard_piece[0], preferred_element_type=jnp.float32
    ) - jnp.einsum("eh,ekm->hkm", sin_rows, shard_piece[1], preferred_element_type=jnp.float32)
    imag_part = jnp.einsum(
        "eh,ekm->hkm", sin_rows, shard_piece[0], preferred_element_type=jnp.float32
    ) + jnp.einsum("eh,ekm->hkm", cos_rows, shard_piece[1], preferred_element_type=jnp.float32)
    totals = jnp.stack([real_part, imag_part])
    image_out = (totals * (1.0 / math.sqrt(E))).astype(jnp.bfloat16)
    return image_out


def trig_pair(row_ids, col_ids, length, split=32):
    fine = jnp.arange(split, dtype=jnp.int32)

    def small(factor):
        product = (factor[:, None] * col_ids[None, :]) % length
        angle = product.astype(jnp.float32) * (2.0 * math.pi / length)
        return jnp.cos(angle), jnp.sin(angle)

    block = row_ids.shape[0] // split
    starts = row_ids.reshape(block, split)[:, 0]
    low_cos, low_sin = small(fine)
    high_cos, high_sin = small(starts)
    low_cos, low_sin, high_cos, high_sin = lax.optimization_barrier(
        (low_cos, low_sin, high_cos, high_sin)
    )
    shape = (block * split, col_ids.shape[0])
    cos_t = high_cos[:, None] * low_cos[None] - high_sin[:, None] * low_sin[None]
    sin_t = high_sin[:, None] * low_cos[None] + high_cos[:, None] * low_sin[None]
    return (
        cos_t.reshape(shape).astype(jnp.bfloat16),
        sin_t.reshape(shape).astype(jnp.bfloat16),
    )


def cost(flops, moved):
    return pl.CostEstimate(flops=int(flops), bytes_accessed=int(moved), transcendentals=0)


def params():
    return pltpu.CompilerParams(vmem_limit_bytes=48 * 1024 * 1024)


def weights_body(off_ref, cnt_ref, tap_ref, w_ref):
    rows = 16

    @pl.loop(0, off_ref.shape[0] // rows)
    def _(step):
        at = pl.ds(pl.multiple_of(step * rows, rows), rows)
        off = off_ref[at, :]
        cnt = cnt_ref[at, :]
        taps = [
            jnp.where(t < cnt, tap_ref[t, at, :].astype(jnp.float32), 0.0) for t in range(KT)
        ]
        for d in range(2 * HW + 1):
            rel = (d - HW) - off
            acc = jnp.zeros(off.shape, jnp.float32)
            for t in range(KT):
                acc = jnp.where(rel == t, taps[t], acc)
            w_ref[d, at, :] = acc.astype(jnp.bfloat16)


def band_weights(band_offset, tap_count, tap_weight):
    cols, freqs = band_offset.shape
    taps = 2 * HW + 1
    return pl.pallas_call(
        weights_body,
        out_shape=jax.ShapeDtypeStruct((taps, cols, freqs), jnp.bfloat16),
        grid=(freqs // LANES,),
        in_specs=[
            pl.BlockSpec((cols, LANES), lambda i: (0, i)),
            pl.BlockSpec((cols, LANES), lambda i: (0, i)),
            pl.BlockSpec((KT, cols, LANES), lambda i: (0, 0, i)),
        ],
        out_specs=pl.BlockSpec((taps, cols, LANES), lambda i: (0, 0, i)),
        compiler_params=params(),
        cost_estimate=cost(10**9, 6 * 10**6),
        name="weights",
    )(band_offset, tap_count, tap_weight)


def interp_body(x_ref, l_ref, r_ref, w_ref, o_ref, buf):
    cuts = x_ref.shape[1]
    cols = x_ref.shape[2]
    rows = 16
    for c in range(2):
        for e in range(cuts):
            p = c * cuts + e
            buf[p, 0:HW, :] = l_ref[c, e].astype(jnp.float32)
            buf[p, HW : HW + cols, :] = x_ref[c, e].astype(jnp.float32)
            buf[p, HW + cols : 2 * HW + cols, :] = r_ref[c, e].astype(jnp.float32)

    @pl.loop(0, cols // rows)
    def _(step):
        base = pl.multiple_of(step * rows, rows)
        weights = [
            w_ref[d, pl.ds(base, rows), :].astype(jnp.float32) for d in range(2 * HW + 1)
        ]
        for c in range(2):
            for e in range(cuts):
                p = c * cuts + e
                acc = weights[0] * buf[p, pl.ds(base, rows), :]
                for d in range(1, 2 * HW + 1):
                    acc = acc + weights[d] * buf[p, pl.ds(base + d, rows), :]
                o_ref[c, e, pl.ds(base, rows), :] = acc.astype(jnp.bfloat16)


def interpolate(polar, left, right, weights, first, cuts):
    _, _, cols, freqs = polar.shape
    taps = 2 * HW + 1
    chunk = first // cuts
    return pl.pallas_call(
        interp_body,
        out_shape=jax.ShapeDtypeStruct((2, cuts, cols, freqs), jnp.bfloat16),
        grid=(freqs // LANES,),
        in_specs=[
            pl.BlockSpec((2, cuts, cols, LANES), lambda i: (0, chunk, 0, i)),
            pl.BlockSpec((2, cuts, HW, LANES), lambda i: (0, chunk, 0, i)),
            pl.BlockSpec((2, cuts, HW, LANES), lambda i: (0, chunk, 0, i)),
            pl.BlockSpec((taps, cols, LANES), lambda i: (0, 0, i)),
        ],
        out_specs=pl.BlockSpec((2, cuts, cols, LANES), lambda i: (0, 0, 0, i)),
        scratch_shapes=[pltpu.VMEM((2 * cuts, cols + 2 * HW, LANES), jnp.float32)],
        compiler_params=params(),
        cost_estimate=cost(10**9, 6 * 10**6),
        name="interp",
    )(polar, left, right, weights)


def range_body(own_ref, par_ref, tab_ref, *rest):
    outs = rest[:-1]
    xs = rest[-1]
    half = own_ref.shape[3]
    for c in range(2):
        xs[c, :, 0:half] = own_ref[c, 0]
        xs[c, :, half:] = par_ref[c, 0]
    dims = (((1,), (1,)), ((), ()))
    table = tab_ref[...]
    from_real = lax.dot_general(table, xs[0], dims, preferred_element_type=jnp.float32)
    from_imag = lax.dot_general(table, xs[1], dims, preferred_element_type=jnp.float32)
    bins = table.shape[0] // 2
    scale = 1.0 / math.sqrt(F)
    real = ((from_real[:bins] - from_imag[bins:]) * scale).astype(jnp.bfloat16)
    imag = ((from_real[bins:] + from_imag[:bins]) * scale).astype(jnp.bfloat16)
    early = outs[-1]
    pieces = len(outs) - 1
    size = bins // pieces
    late = outs[0].shape[2]
    for s in range(pieces):
        for c, part in enumerate((real, imag)):
            outs[s][c, 0] = part[s * size : s * size + late]
            early[c, 0, s] = part[s * size + late : (s + 1) * size]


def range_transform(own, partner, table, pieces, early):
    _, cuts, cols, half = own.shape
    late = table.shape[0] // 2 // pieces - early
    spec = pl.BlockSpec((2, 1, cols, half), lambda i: (0, i, 0, 0))
    return pl.pallas_call(
        range_body,
        out_shape=[jax.ShapeDtypeStruct((2, cuts, late, cols), jnp.bfloat16)] * pieces
        + [jax.ShapeDtypeStruct((2, cuts, pieces, early, cols), jnp.bfloat16)],
        grid=(cuts,),
        in_specs=[spec, spec, pl.BlockSpec(table.shape, lambda i: (0, 0))],
        out_specs=[pl.BlockSpec((2, 1, late, cols), lambda i: (0, i, 0, 0))] * pieces
        + [pl.BlockSpec((2, 1, pieces, early, cols), lambda i: (0, i, 0, 0, 0))],
        scratch_shapes=[pltpu.VMEM((2, cols, 2 * half), jnp.bfloat16)],
        compiler_params=params(),
        cost_estimate=cost(4 * table.size * cuts * cols, 6 * 10**6),
        name="range_dft",
    )(own, partner, table)


def cross_body(pieces, *refs):
    cos_ref, sin_ref = refs[pieces : pieces + 2]
    out_ref, lhs = refs[-2:]
    _, cuts, bins, cols = refs[0].shape

    @pl.when(pl.program_id(0) == 0)
    def _():
        for s in range(pieces):
            block = refs[s][...].reshape(2 * cuts * bins, cols)
            lhs[:, s * cols : (s + 1) * cols] = block

    left = lhs[...]
    by_cos = jnp.dot(left, cos_ref[...], preferred_element_type=jnp.float32)
    by_sin = jnp.dot(left, sin_ref[...], preferred_element_type=jnp.float32)
    rows = cuts * bins
    scale = 1.0 / math.sqrt(A)
    shape = (cuts, bins, cos_ref.shape[1])
    real = (by_cos[:rows] - by_sin[rows:]) * scale
    imag = (by_sin[:rows] + by_cos[rows:]) * scale
    out_ref[0] = real.astype(jnp.bfloat16).reshape(shape)
    out_ref[1] = imag.astype(jnp.bfloat16).reshape(shape)


def cross_transform(pieces, cos_a, sin_a, image=None, total=None, at=0):
    _, cuts, bins, cols = pieces[0].shape
    depth, width = cos_a.shape
    tile = 256
    whole = pl.BlockSpec((2, cuts, bins, cols), lambda i: (0, 0, 0, 0))
    table = pl.BlockSpec((depth, tile), lambda i: (0, i))
    count = len(pieces)
    held = [] if image is None else [image]
    return pl.pallas_call(
        functools.partial(cross_body, count),
        out_shape=jax.ShapeDtypeStruct((2, cuts, total or bins, width), jnp.bfloat16),
        grid=(width // tile,),
        in_specs=[whole] * count + [table, table] + [pl.BlockSpec(memory_space=pl.ANY)] * len(held),
        out_specs=pl.BlockSpec((2, cuts, bins, tile), lambda i: (0, 0, at // bins, i)),
        scratch_shapes=[pltpu.VMEM((2 * cuts * bins, depth), jnp.bfloat16)],
        input_output_aliases={count + 2: 0} if held else {},
        compiler_params=params(),
        cost_estimate=cost(8 * cuts * bins * depth * width, 8 * 10**6),
        name="cross_dft",
    )(*pieces, cos_a, sin_a, *held)


def height_body(count, *refs):
    tab_ref = refs[count]
    out_ref, data = refs[-2:]
    at = 0
    for ref in refs[:count]:
        parts, cuts, rows, width = ref.shape
        size = parts * cuts * rows
        data[at : at + size, :] = ref[...].reshape(size, width)
        at += size
    parts, heights, rows, width = out_ref.shape
    scale = 1.0 / math.sqrt(E)
    tile = 256
    for t in range(width // tile):
        cols = slice(t * tile, (t + 1) * tile)
        total = jnp.dot(tab_ref[...], data[:, cols], preferred_element_type=jnp.float32)
        total = (total * scale).astype(jnp.bfloat16)
        out_ref[:, :, :, cols] = total.reshape(parts, heights, rows, tile)


def height_transform(chunks, table, image, bins):
    _, heights, _, width = image.shape
    count = len(chunks)
    specs = [
        pl.BlockSpec((2, x.shape[1], GROUP, width), lambda i: (0, 0, i, 0)) for x in chunks
    ]
    return pl.pallas_call(
        functools.partial(height_body, count),
        out_shape=jax.ShapeDtypeStruct(image.shape, jnp.bfloat16),
        grid=(bins // GROUP,),
        in_specs=specs
        + [pl.BlockSpec(table.shape, lambda i: (0, 0)), pl.BlockSpec(memory_space=pl.ANY)],
        input_output_aliases={count + 1: 0},
        out_specs=pl.BlockSpec((2, heights, GROUP, width), lambda i: (0, 0, i, 0)),
        scratch_shapes=[pltpu.VMEM((table.shape[1], width), jnp.bfloat16)],
        compiler_params=params(),
        cost_estimate=cost(2 * table.size * width * (bins // GROUP), 2 * 10**7),
        name="height_dft",
    )(*chunks, table, image)


def early_body(count, *refs):
    tab_ref = refs[count]
    outs = refs[count + 1 : -1]
    data = refs[-1]
    scale = 1.0 / math.sqrt(E)
    for s, out_ref in enumerate(outs):
        at = 0
        for ref in refs[:count]:
            parts, cuts, _, rows, width = ref.shape
            size = parts * cuts * rows
            data[s, at : at + size, :] = ref[:, :, s].reshape(size, width)
            at += size
        total = jnp.dot(tab_ref[...], data[s], preferred_element_type=jnp.float32)
        out_ref[...] = (total * scale).astype(jnp.bfloat16).reshape(out_ref.shape)


def early_heights(chunks, table, heights, group):
    _, _, pieces, _, cols = chunks[0].shape
    count = len(chunks)
    specs = [
        pl.BlockSpec((2, x.shape[1], pieces, GROUP, cols), lambda i: (0, 0, 0, group, 0))
        for x in chunks
    ]
    out = (2, heights, GROUP, cols)
    return pl.pallas_call(
        functools.partial(early_body, count),
        out_shape=[jax.ShapeDtypeStruct(out, jnp.bfloat16)] * pieces,
        grid=(1,),
        in_specs=specs + [pl.BlockSpec(table.shape, lambda i: (0, 0))],
        out_specs=[pl.BlockSpec(out, lambda i: (0, 0, 0, 0))] * pieces,
        scratch_shapes=[pltpu.VMEM((pieces, table.shape[1], cols), jnp.bfloat16)],
        compiler_params=params(),
        cost_estimate=cost(2 * table.size * cols * pieces, 4 * 10**6),
        name="early_height",
    )(*chunks, table)


def height_table(height_ids, elev_starts):
    columns = []
    for start in elev_starts:
        first = 0
        for cuts in CUTS:
            ids = start + first + jnp.arange(cuts, dtype=jnp.int32)
            cos_e, sin_e = table_pair(height_ids, ids, E)
            columns.append(jnp.concatenate([cos_e, sin_e]))
            columns.append(jnp.concatenate([-sin_e, cos_e]))
            first += cuts
    small = jnp.concatenate(columns, axis=1)
    rows, cols = small.shape
    row = jnp.arange(rows * GROUP, dtype=jnp.int32)
    col = jnp.arange(cols * GROUP, dtype=jnp.int32)
    take_row = (row[:, None] // GROUP == jnp.arange(rows)[None]).astype(jnp.bfloat16)
    take_col = (jnp.arange(cols)[:, None] == col[None] // GROUP).astype(jnp.bfloat16)
    wide = jnp.dot(jnp.dot(take_row, small), take_col)
    same = row[:, None] % GROUP == col[None] % GROUP
    return jnp.where(same, wide, jnp.zeros((), jnp.bfloat16))


def ring(pieces, axis):
    count = len(pieces)
    out = [pieces[0]]
    for s in range(1, count):
        out.append(
            lax.ppermute(pieces[s], axis, [(i, (i + s) % count) for i in range(count)])
        )
    return out


def kernel_order():
    count = len(CUTS)
    order = [("interp", 0)]
    for chunk in range(1, count):
        order += [("interp", chunk), ("range", chunk - 1)]
    order += [("range", count - 1)]
    order += [("cross", chunk) for chunk in range(BEFORE)]
    order += [("early", group) for group in range(EARLY)]
    order += [("cross", chunk) for chunk in range(BEFORE, count)]
    order += [("last", group) for group in range(EARLY - 1)]
    order += [("height", 0), ("last", EARLY - 1)]
    return order


def pipelined(polar, band_offset, tap_count, tap_weight):
    _, e_here, col_count, freq_count = polar.shape
    az_count = lax.axis_size("az")
    fq_count = lax.axis_size("fq")
    el_count = lax.axis_size("el")
    az, fq, el = (lax.axis_index(name) for name in ("az", "fq", "el"))
    bins = F // (fq_count * az_count)
    heights = E // el_count
    early = EARLY * GROUP
    late = bins - early
    ends = az_count - 1
    left = lax.ppermute(
        polar[:, :, col_count - HW :], "az", [(i, i + 1) for i in range(ends)]
    )
    right = lax.ppermute(polar[:, :, :HW], "az", [(i + 1, i) for i in range(ends)])
    weights = band_weights(band_offset, tap_count, tap_weight)

    shifts = jnp.arange(az_count, dtype=jnp.int32)
    targets = (az + shifts) % az_count
    local = jnp.arange(bins, dtype=jnp.int32)
    range_ids = ((targets[:, None] * fq_count + fq) * bins + local[None]).reshape(-1)
    f_local = jnp.arange(freq_count, dtype=jnp.int32)
    freq_ids = jnp.concatenate([fq * freq_count + f_local, (1 - fq) * freq_count + f_local])
    cos_f, sin_f = trig_pair(range_ids, freq_ids, F)
    range_table = jnp.concatenate([cos_f, sin_f])

    firsts = [sum(CUTS[:c]) for c in range(len(CUTS))]
    mixed, pieces, partners = {}, {}, {}
    ahead = [[] for _ in range(el_count)]
    passed = [[] for _ in range(el_count)]
    early_blocks = {}
    image = None
    last = None

    for kind, n in kernel_order():
        if kind == "interp":
            gate = hold(weights, last)
            last = interpolate(polar, left, right, gate, firsts[n], CUTS[n])
            mixed[n] = last
        elif kind == "range":
            gate = hold(range_table, last)
            outs = range_transform(mixed[n], partners[n], gate, az_count, early)
            last = outs[0]
        elif kind == "cross":
            if n == 0:
                az_late, el_late = hold((az, el), last)
                cos_a, sin_a = azimuth_tables(az_late, az_count, col_count)
                height_ids = el_late * heights + jnp.arange(heights, dtype=jnp.int32)
                starts = [(el_late - s) % el_count * e_here for s in range(el_count)]
                table = height_table(height_ids, starts)
            own = [hold(pieces[n][0], last)] + pieces[n][1:]
            last = cross_transform(own, cos_a, sin_a)
        elif kind == "early":
            blocks = early_heights(sum(ahead, []), hold(table, last), heights, n)
            last = blocks[0]
        elif kind == "height":
            image = height_transform(sum(passed, []), table, image, late)
        else:
            own = early_blocks[n]
            if n == 0:
                own = [hold(own[0], last)] + own[1:]
            image = cross_transform(
                own, cos_a, sin_a, image, bins, late + n * GROUP
            )
        if kind == "interp":
            partners[n] = ring([last, last], "fq")[1]
        elif kind == "range":
            pieces[n] = ring(outs[:-1], "az")
            for s, block in enumerate(ring([outs[-1]] * el_count, "el")):
                ahead[s].append(block)
        elif kind == "cross":
            block = hold(last, ahead[-1][-1]) if n < BEFORE else last
            for s, part in enumerate(ring([block] * el_count, "el")):
                passed[s].append(part)
        elif kind == "early":
            early_blocks[n] = ring(blocks, "az")
    return image


def azimuth_tables(az, az_count, col_count):
    sources = (az - jnp.arange(az_count, dtype=jnp.int32)) % az_count
    col_local = jnp.arange(col_count, dtype=jnp.int32)
    azim_ids = (sources[:, None] * col_count + col_local[None]).reshape(-1)
    return trig_pair(azim_ids, jnp.arange(A, dtype=jnp.int32), A)


def hold(value, last):
    return value if last is None else lax.optimization_barrier((value, last))[0]


def pick(polar, band_offset, tap_count, tap_weight):
    _, e_here, col_count, freq_count = polar.shape
    bins = F // (lax.axis_size("fq") * lax.axis_size("az"))
    fits = (
        lax.axis_size("fq") == 2
        and lax.axis_size("az") <= 4
        and e_here == sum(CUTS)
        and bins % GROUP == 0
        and bins > EARLY * GROUP
        and col_count % LANES == 0
        and freq_count % LANES == 0
    )
    if not fits:
        return on_device(polar, band_offset, tap_count, tap_weight)
    return pipelined(polar, band_offset, tap_count, tap_weight)


def solution(mesh):
    in_specs = (
        P(None, ("grp", "el"), "az", "fq"),
        P("az", "fq"),
        P("az", "fq"),
        P(None, "az", "fq"),
    )
    out_specs = P(None, ("grp", "el"), ("az", "fq"), None)
    return jax.shard_map(
        pick, mesh=mesh, in_specs=in_specs, out_specs=out_specs, check_vma=False
    )
```
